256 devices in a mesh: rows: 64 (over x, z, core), cols: 4 (over y).
Axes of the slice: x: 4, y: 4, z: 8, core: 2. Of those that a mesh axis runs over, the one named last changes fastest.
Arguments:
- panel: float32 [32768, 1024], P('rows'), as said below
- window_block: float32 [32768, 2048], P('rows', 'cols'), may hold values from -6 to 6
- row_live: int32 [64], replicated, may hold values 0 or 1
- window_rows: int32 [4], replicated, may hold values from 2 to 63, as said below
Outputs:
- factor: float32 [32768, 1024], P('rows')
- updated: float32 [32768, 2048], P('rows', 'cols')
The draws below stay inside these ranges and needn't reach their ends.
Inputs may be any that keep to these rules, and one draw needn't show every extreme that they name: `window_rows`: distinct tile rows, none inside the supernode. `row_live`: the value for tile rows below 2 is ignored: those rows are always present. `panel`: the first 1024 rows hold a symmetric positive definite block.
All inputs are finite; a program needn't handle non-finite values.
Results may differ from the reference program's by a relative error of at most 0.0001.
Values sent between devices are 32-bit elements; how exact they have to be, the bound alone decides.
No kernel may reach another device: no remote copies, remote signals or barrier semaphores. Data moves between devices by JAX's collectives and lax.ppermute only.
A program may use at most 128 MiB of HBM per device.

```python
import jax
import jax.numpy as jnp
from jax import lax

B = 512
P_SIZE = 2
NT = 64
NW = 4


def draw_window_rows(key, part):
    pair = jax.random.split(key, 2)
    first = jax.random.randint(pair[0], (NT - P_SIZE,), 0, 1 << 14)
    second = jax.random.randint(pair[1], (NT - P_SIZE,), 0, 1 << 14)
    scores = (first * 16384 + second) % 1048576
    distinct = scores * NT + jnp.arange(NT - P_SIZE)
    values, places = lax.top_k(distinct, NW)
    return (places + P_SIZE).astype(jnp.int32)


def draw_panel(key, part):
    keys = jax.random.split(jax.random.fold_in(key, 5), 5)
    total_rows = NT * B
    width = P_SIZE * B
    reach = max(4.0, width / 48.0)
    base = jax.random.normal(keys[0], (total_rows, width)) * 0.25
    rough = jax.random.normal(keys[1], (width, width)) * (0.15 / width ** 0.5)
    rough = (rough + rough.T) * 0.70710678
    places = jnp.arange(width).astype(jnp.float32)
    distance = jnp.abs(places[:, None] - places[None, :])
    kernel = 0.6 * jnp.exp(-distance / reach)
    diag_vals = jax.random.uniform(keys[2], (width,), minval=0.8, maxval=1.6)
    scales = jnp.exp(jax.random.uniform(keys[4], (width,), minval=jnp.log(0.8), maxval=jnp.log(1.25)))
    head = scales[:, None] * scales[None, :] * (kernel + rough) + jnp.diag(diag_vals)
    head_full = jnp.concatenate([head, jnp.zeros((total_rows - width, width), jnp.float32)], axis=0)
    row_ids = jnp.arange(total_rows)[:, None]
    return jnp.where(row_ids < width, head_full, base).astype(jnp.float32)


def set_ends(array, stream_key, smallest, largest):
    extent = array.shape
    place = [jax.random.randint(jax.random.fold_in(stream_key, axis), (), 0, extent[axis]) for axis in range(len(extent))]
    array = array.at[tuple(place)].set(smallest)
    longest = extent.index(max(extent))
    place[longest] = (place[longest] + 1) % extent[longest]
    return array.at[tuple(place)].set(largest)


def block_levels(rng, shape, pieces, low, largest):
    loudness, own = 1.0, jax.random.fold_in(rng, 6)
    for position, blocks in pieces:
        draws = jnp.exp(jax.random.uniform(jax.random.fold_in(own, position), (blocks,), jnp.float32, low / len(pieces), largest / len(pieces)))
        loudness = loudness * jnp.repeat(draws, shape[position] // blocks).reshape([-1 if axis == position else 1 for axis in range(len(shape))])
    return loudness


def noise(rng, extent, spread, most, cuts=(), dtype=jnp.bfloat16):
    result = spread * jax.random.normal(rng, extent, jnp.float32)
    if cuts:
        result = result * block_levels(rng, extent, cuts, -0.22, 0.18)
    return jnp.clip(result, -most, most).astype(dtype)


def setup_inputs(seed: int = 0) -> dict:
    arg_keys = jax.random.split(jax.random.key(seed), 5)
    return {
        "panel": draw_panel(jax.random.fold_in(arg_keys[4], 71), 0),
        "window_block": noise(arg_keys[1], (NT * B, NW * B), 1.0, 6.0, ((0, 64), (1, 4)), jnp.float32),
        "row_live": set_ends((jax.random.randint(arg_keys[2], (NT,), 0, 4) < 3).astype(jnp.int32), jax.random.fold_in(arg_keys[2], 1), 0, 1),
        "window_rows": draw_window_rows(jax.random.fold_in(arg_keys[4], 71), 0),
    }


def reference(panel, window_block, row_live, window_rows):
    tile_ids = jnp.arange(NT)
    live_flag = jnp.where(tile_ids < P_SIZE, 1, row_live).astype(jnp.float32)
    scaled = panel * jnp.repeat(live_flag, B)[:, None]
    head = scaled[:P_SIZE * B]
    square = jnp.tril(head) + jnp.tril(head, -1).T
    lower = jnp.linalg.cholesky(square)
    solved = lax.linalg.triangular_solve(lower, scaled, left_side=False, lower=True, transpose_a=True)
    factor = jnp.concatenate([lower, solved[P_SIZE * B:]], axis=0)
    columns = []
    for window in range(NW):
        start = (window_rows[window] * B).astype(jnp.int32)
        target_row = lax.dynamic_slice_in_dim(factor, start, B, 0)
        block_now = window_block[:, window * B:(window + 1) * B]
        product = lax.dot_general(factor, target_row, (((1,), (1,)), ((), ())), precision=lax.Precision.HIGHEST)
        columns.append(block_now - product)
    return (factor, jnp.concatenate(columns, axis=1))
```

```python
import functools

import jax
import jax.numpy as jnp
from jax import lax
from jax.experimental import pallas as pl
from jax.experimental.pallas import tpu as pltpu
from jax.sharding import PartitionSpec as P

F32 = jnp.float32
B = 512
NB = 128
NX, NZ, NY = 4, 8, 4
VMEM_LIMIT = 56 << 20
CONTRACT = (((1,), (1,)), ((), ()))


def lanes(v, j):
    return jnp.broadcast_to(v[:, j : j + 1], (8, NB))


def sublanes(v, s):
    return jnp.broadcast_to(v[s : s + 1, :], (8, NB))


def factor_block(V):
    sub = lax.broadcasted_iota(jnp.int32, (8, NB), 0)
    lane = lax.broadcasted_iota(jnp.int32, (8, NB), 1)
    groups = NB // 8
    E = [jnp.where(lane == sub + 8 * k, 1.0, 0.0).astype(F32) for k in range(groups)]
    upper, inverse = [], []
    for k in range(groups):
        R = [sublanes(V[k], a) for a in range(8)]
        Q = [sublanes(E[k], a) for a in range(8)]
        s = {(a, b): lanes(R[a], 8 * k + b) for a in range(8) for b in range(a + 1)}
        C = {kk: [lanes(V[kk], 8 * k + b) for b in range(8)] for kk in range(k + 1, groups)}
        for b in range(8):
            inv = lax.rsqrt(s[b, b])
            l = {a: s[a, b] * inv for a in range(b + 1, 8)}
            for a in range(b + 1, 8):
                for c in range(b + 1, a + 1):
                    s[a, c] = s[a, c] - l[a] * l[c]
            R[b] = R[b] * inv
            Q[b] = Q[b] * inv
            for a in range(b + 1, 8):
                R[a] = R[a] - l[a] * R[b]
                Q[a] = Q[a] - l[a] * Q[b]
            for kk in C:
                C[kk][b] = C[kk][b] * inv
                for a in range(b + 1, 8):
                    C[kk][a] = C[kk][a] - C[kk][b] * l[a]
        for kk in C:
            for b in range(8):
                V[kk] = V[kk] - C[kk][b] * R[b]
                E[kk] = E[kk] - C[kk][b] * Q[b]
        u, x = R[0], Q[0]
        for a in range(1, 8):
            u = jnp.where(sub == a, R[a], u)
            x = jnp.where(sub == a, Q[a], x)
        upper.append(jnp.where(lane >= sub + 8 * k, u, 0.0))
        inverse.append(x)
    return upper, inverse


def halves(a):
    hi = a.astype(jnp.bfloat16)
    return hi, (a - hi.astype(F32)).astype(jnp.bfloat16)


def mul_t(a, b):
    ah, al = halves(a)
    bh, bl = halves(b)
    d = functools.partial(lax.dot_general, dimension_numbers=CONTRACT, preferred_element_type=F32)
    return d(ah, bh) + (d(ah, bl) + d(al, bh))


def mirrored(d):
    r = lax.broadcasted_iota(jnp.int32, (NB, NB), 0)
    c = lax.broadcasted_iota(jnp.int32, (NB, NB), 1)
    return jnp.where(r >= c, d, d.T)


def tall_factor(a_ref, f_ref, dinv_ref, d_ref):
    m, n = a_ref.shape
    nb = n // NB
    for k in range(nb):
        o = k * NB
        a_ref[o : o + NB, o : o + NB] = mirrored(a_ref[o : o + NB, o : o + NB])
    d_ref[...] = a_ref[0:NB, 0:NB]

    def body(k, carry):
        V = [d_ref[8 * i : 8 * i + 8, :] for i in range(NB // 8)]
        upper, inverse = factor_block(V)
        low = jnp.concatenate(upper, 0).T
        X = jnp.concatenate(inverse, 0)
        dinv_ref[k] = X

        def branch(kk):
            def run():
                o = NB * kk
                e = o + NB
                f_ref[o:e, o:e] = low
                Lp = mul_t(a_ref[e:, o:e], X)
                f_ref[e:, o:e] = Lp
                if e < n:
                    f_ref[o:e, e:] = jnp.zeros((NB, n - e), F32)
                    T = a_ref[e:, e:] - mul_t(Lp, Lp[: n - e])
                    a_ref[e:, e:] = T
                    d_ref[...] = T[:NB, :NB]
                return 0

            return run

        return lax.switch(k, [branch(kk) for kk in range(nb)]) + carry

    lax.fori_loop(0, nb, body, 0)


def place_static(meta, own_ref, other_ref, core, put):
    x, y, mine = meta[0], meta[3], meta[2]
    rows = own_ref.shape[2]
    for dy in range(NY):
        for dx in range(NX):
            row = (lax.rem(y - dy + NY, NY) * NX + lax.rem(x - dx + NX, NX)) * rows
            row = pl.multiple_of(row, 8)

            @pl.when(mine == core)
            def _():
                put(row, rows, own_ref[dy, dx])

            @pl.when(mine != core)
            def _():
                put(row, rows, other_ref[dy, dx])


def kernel_a(meta, own_ref, other_ref, panel_ref, f_ref, dinv_ref, a_ref, d_ref):
    def put0(row, rows, value):
        a_ref[pl.ds(row, rows), :] = value

    def put1(row, rows, value):
        a_ref[pl.ds(row + B, rows), :] = value

    place_static(meta, own_ref, other_ref, 0, put0)
    place_static(meta, own_ref, other_ref, 1, put1)
    a_ref[2 * B :, :] = panel_ref[...] * meta[5].astype(F32)
    tall_factor(a_ref, f_ref, dinv_ref, d_ref)


def kernel_b(meta, own_ref, other_ref, panel_ref, f0_ref, f1_ref, dinv_ref, factor_ref, a_ref, d_ref):
    def put0(row, rows, value):
        a_ref[pl.ds(row, rows), :] = value

    def put1(row, rows, value):
        a_ref[pl.ds(row + B // 2, rows), :] = value

    place_static(meta, own_ref, other_ref, 0, put0)
    place_static(meta, own_ref, other_ref, 1, put1)
    a_ref[B:, :] = panel_ref[...] * meta[5].astype(F32)
    low = f0_ref[B : 2 * B, :]
    a_ref[...] = a_ref[...] - mul_t(f0_ref[B:, :], low)
    tall_factor(a_ref, f1_ref, dinv_ref, d_ref)
    row = meta[4]

    @pl.when(row == 0)
    def _():
        factor_ref[:, :B] = f0_ref[:B, :]
        factor_ref[:, B:] = jnp.zeros((B, B), F32)

    @pl.when(row == 1)
    def _():
        factor_ref[:, :B] = f0_ref[B : 2 * B, :]
        factor_ref[:, B:] = f1_ref[:B, :]

    @pl.when(row > 1)
    def _():
        factor_ref[:, :B] = f0_ref[2 * B :, :]
        factor_ref[:, B:] = f1_ref[B:, :]


def kernel_c(meta, own_ref, other_ref, f0_ref, f1_ref, d0_ref, d1_ref, factor_ref, window_ref, out_ref, s_ref):
    x, z, mine = meta[0], meta[1], meta[2]
    live = meta[6].astype(F32)
    for dz in range(NZ):
        for dx in range(NX):
            k = lax.rem(x - dx + NX, NX) * NZ + lax.rem(z - dz + NZ, NZ)
            s_ref[pl.ds(pl.multiple_of((2 * k + mine) * 8, 8), 8), :] = own_ref[dz, dx] * live
            s_ref[pl.ds(pl.multiple_of((2 * k + 1 - mine) * 8, 8), 8), :] = other_ref[dz, dx] * live
    for k in range(4):
        o, e = k * NB, k * NB + NB
        X = mul_t(s_ref[:, o:e], d0_ref[k])
        s_ref[:, o:e] = X
        s_ref[:, e:] = s_ref[:, e:] - mul_t(X, f0_ref[e : 2 * B, o:e])
    for k in range(4):
        o, e = k * NB, k * NB + NB
        X = mul_t(s_ref[:, B + o : B + e], d1_ref[k])
        s_ref[:, B + o : B + e] = X
        if e < B:
            s_ref[:, B + e :] = s_ref[:, B + e :] - mul_t(X, f1_ref[e:B, o:e])
    out_ref[...] = window_ref[...] - mul_t(factor_ref[...], s_ref[...])


SMEM = pl.BlockSpec(memory_space=pltpu.SMEM)
VM = pl.BlockSpec(memory_space=pltpu.VMEM)


def call(kernel, outs, scratch, *args):
    return pl.pallas_call(
        kernel,
        out_shape=[jax.ShapeDtypeStruct(s, F32) for s in outs],
        in_specs=[SMEM] + [VM] * (len(args) - 1),
        out_specs=[VM] * len(outs),
        scratch_shapes=[pltpu.VMEM(s, F32) for s in scratch],
        compiler_params=pltpu.CompilerParams(vmem_limit_bytes=VMEM_LIMIT),
    )(*args)


def rid(x, z, c):
    return (x * NZ + z) * 2 + c


def move(v, keep, to):
    pairs = [
        (rid(x, z, c), rid(*to(x, z, c)))
        for x in range(NX)
        for z in range(NZ)
        for c in range(2)
        if keep(x, z, c)
    ]
    return lax.ppermute(v, "rows", pairs)


def always(x, z, c):
    return True


def by_x(v, d, keep=always):
    return move(v, keep, lambda x, z, c: ((x + d) % NX, z, c))


def by_z(v, d, keep=always):
    return move(v, keep, lambda x, z, c: (x, (z + d) % NZ, c))


def swap_core(v):
    return move(v, always, lambda x, z, c: (x, z, 1 - c))


def gather_x(v):
    return jnp.stack([v] + [by_x(v, d) for d in range(1, NX)])


def spread_static(v, x, z, y):
    quarter = lax.dynamic_slice_in_dim(v, y * (v.shape[0] // NY), v.shape[0] // NY, 0)
    pieces = quarter.reshape(NX, v.shape[0] // (NX * NY), v.shape[1])
    root = (x == 0) & (z == 0)

    def at_root(x, z, c):
        return x == 0 and z == 0

    piece = jnp.where(root, pieces[0], 0.0)
    piece = piece + sum(by_x(pieces[d], d, at_root) for d in range(1, NX))

    def first(x, z, c):
        return z == 0

    piece = piece + sum(by_z(piece, d, first) for d in (2, 4, 6))
    piece = piece + by_z(piece, 1, lambda x, z, c: z % 2 == 0)
    part = gather_x(piece)
    own = jnp.stack([part] + [lax.ppermute(part, "cols", [(i, (i + d) % NY) for i in range(NY)]) for d in range(1, NY)])
    return own, swap_core(own)


def shards(panel, window_block, row_live, window_rows):
    row = lax.axis_index("rows")
    y = lax.axis_index("cols")
    x, z, core = row // (2 * NZ), (row // 2) % NZ, row % 2
    target = window_rows[y]
    live = jnp.where(row < 2, 1, row_live[row])
    meta = jnp.stack([x, z, core, y, row, live, row_live[target], 0]).astype(jnp.int32)

    first = panel[:, :B]
    half = jnp.where(core == 0, lax.ppermute(panel[: B // 2, B:], "rows", [(1, 0)]), panel[B // 2 :, B:])
    own1, other1 = spread_static(first, x, z, y)
    own2, other2 = spread_static(half, x, z, y)

    width = 2 * B // NY
    mine = lax.dynamic_slice_in_dim(panel, y * width, width, 1).reshape(64, 8, width)
    parts = lax.all_to_all(mine, "rows", 0, 0)
    chosen = jnp.stack([lax.dynamic_index_in_dim(parts, window_rows[c], 0, keepdims=False) for c in range(NY)])
    quarters = lax.all_to_all(chosen, "cols", 0, 0)
    shard = jnp.concatenate([quarters[q] for q in range(NY)], axis=1)
    shard = gather_x(shard)
    t_own = jnp.stack([shard] + [by_z(shard, d) for d in range(1, NZ)])
    t_other = swap_core(t_own)

    f0, d0 = call(kernel_a, [(3 * B, B), (4, NB, NB)], [(3 * B, B), (NB, NB)], meta, own1, other1, panel[:, :B])
    f1, d1, factor = call(
        kernel_b,
        [(2 * B, B), (4, NB, NB), (B, 2 * B)],
        [(2 * B, B), (NB, NB)],
        meta, own2, other2, panel[:, B:], f0,
    )
    (updated,) = call(
        kernel_c, [(B, B)], [(B, 2 * B)], meta, t_own, t_other, f0, f1, d0, d1, factor, window_block
    )
    return factor, updated


def solution(mesh):
    in_specs = (P("rows", None), P("rows", "cols"), P(), P())
    out_specs = (P("rows", None), P("rows", "cols"))
    return jax.shard_map(shards, mesh=mesh, in_specs=in_specs, out_specs=out_specs, check_vma=False)
```

```python
import functools

import jax
import jax.numpy as jnp
from jax import lax
from jax.experimental import pallas as pl
from jax.experimental.pallas import tpu as pltpu
from jax.sharding import PartitionSpec as P

F32 = jnp.float32
B = 512
NB = 128
NX, NZ, NY = 4, 8, 4
VMEM_LIMIT = 56 << 20
CONTRACT = (((1,), (1,)), ((), ()))


def lanes(v, j):
    return jnp.broadcast_to(v[:, j : j + 1], (8, NB))


def sublanes(v, s):
    return jnp.broadcast_to(v[s : s + 1, :], (8, NB))


def factor_block(V):
    sub = lax.broadcasted_iota(jnp.int32, (8, NB), 0)
    lane = lax.broadcasted_iota(jnp.int32, (8, NB), 1)
    groups = NB // 8
    E = [jnp.where(lane == sub + 8 * k, 1.0, 0.0).astype(F32) for k in range(groups)]
    upper, inverse = [], []
    for k in range(groups):
        R = [sublanes(V[k], a) for a in range(8)]
        Q = [sublanes(E[k], a) for a in range(8)]
        s = {(a, b): lanes(R[a], 8 * k + b) for a in range(8) for b in range(a + 1)}
        C = {kk: [lanes(V[kk], 8 * k + b) for b in range(8)] for kk in range(k + 1, groups)}
        for b in range(8):
            inv = lax.rsqrt(s[b, b])
            l = {a: s[a, b] * inv for a in range(b + 1, 8)}
            for a in range(b + 1, 8):
                for c in range(b + 1, a + 1):
                    s[a, c] = s[a, c] - l[a] * l[c]
            R[b] = R[b] * inv
            Q[b] = Q[b] * inv
            for a in range(b + 1, 8):
                R[a] = R[a] - l[a] * R[b]
                Q[a] = Q[a] - l[a] * Q[b]
            for kk in C:
                C[kk][b] = C[kk][b] * inv
                for a in range(b + 1, 8):
                    C[kk][a] = C[kk][a] - C[kk][b] * l[a]
        for kk in C:
            for b in range(8):
                V[kk] = V[kk] - C[kk][b] * R[b]
                E[kk] = E[kk] - C[kk][b] * Q[b]
        u, x = R[0], Q[0]
        for a in range(1, 8):
            u = jnp.where(sub == a, R[a], u)
            x = jnp.where(sub == a, Q[a], x)
        upper.append(jnp.where(lane >= sub + 8 * k, u, 0.0))
        inverse.append(x)
    return upper, inverse


def halves(a):
    hi = a.astype(jnp.bfloat16)
    return hi, (a - hi.astype(F32)).astype(jnp.bfloat16)


def mul_t(a, b):
    ah, al = halves(a)
    bh, bl = halves(b)
    d = functools.partial(lax.dot_general, dimension_numbers=CONTRACT, preferred_element_type=F32)
    return d(ah, bh) + (d(ah, bl) + d(al, bh))


def mirrored(d):
    r = lax.broadcasted_iota(jnp.int32, (NB, NB), 0)
    c = lax.broadcasted_iota(jnp.int32, (NB, NB), 1)
    return jnp.where(r >= c, d, d.T)


def tall_factor(a_ref, f_ref, dinv_ref, d_ref):
    m, n = a_ref.shape
    nb = n // NB
    for k in range(nb):
        o = k * NB
        a_ref[o : o + NB, o : o + NB] = mirrored(a_ref[o : o + NB, o : o + NB])
    d_ref[...] = a_ref[0:NB, 0:NB]

    def body(k, carry):
        V = [d_ref[8 * i : 8 * i + 8, :] for i in range(NB // 8)]
        upper, inverse = factor_block(V)
        low = jnp.concatenate(upper, 0).T
        X = jnp.concatenate(inverse, 0)
        dinv_ref[k] = X

        def branch(kk):
            def run():
                o = NB * kk
                e = o + NB
                f_ref[o:e, o:e] = low
                Lp = mul_t(a_ref[e:, o:e], X)
                f_ref[e:, o:e] = Lp
                if e < n:
                    f_ref[o:e, e:] = jnp.zeros((NB, n - e), F32)
                    T = a_ref[e:, e:] - mul_t(Lp, Lp[: n - e])
                    a_ref[e:, e:] = T
                    d_ref[...] = T[:NB, :NB]
                return 0

            return run

        return lax.switch(k, [branch(kk) for kk in range(nb)]) + carry

    lax.fori_loop(0, nb, body, 0)


def place(meta, own_ref, other_ref, m_ref):
    y, mine = meta[3], meta[2]
    rows = own_ref.shape[1]
    for dy in range(NY):
        row = pl.multiple_of(lax.rem(y - dy + NY, NY) * rows, 8)
        m_ref[mine, pl.ds(row, rows), :] = own_ref[dy]
        m_ref[1 - mine, pl.ds(row, rows), :] = other_ref[dy]


H = B // 2


def kernel_a(meta, own_ref, other_ref, panel_ref, f_ref, dinv_ref, m_ref, a_ref, d_ref):
    place(meta, own_ref, other_ref, m_ref)
    a_ref[:H, :H] = m_ref[0, :H, :]
    a_ref[:H, H:] = jnp.zeros((H, H), F32)
    a_ref[H:B, :H] = m_ref[0, H : 2 * H, :]
    a_ref[H:B, H:] = m_ref[0, 2 * H : 3 * H, :]
    for i in range(2):
        for j in range(2):
            o = (2 * i + j) * H
            a_ref[B + i * H : B + (i + 1) * H, j * H : (j + 1) * H] = m_ref[1, o : o + H, :]
    a_ref[2 * B :, :] = panel_ref[...] * meta[5].astype(F32)
    tall_factor(a_ref, f_ref, dinv_ref, d_ref)


def kernel_b(meta, own_ref, other_ref, panel_ref, f0_ref, f1_ref, dinv_ref, factor_ref, m_ref, a_ref, d_ref):
    place(meta, own_ref, other_ref, m_ref)
    a_ref[:H, :H] = m_ref[1, 4 * H :, :]
    a_ref[:H, H:] = jnp.zeros((H, H), F32)
    a_ref[H:B, :H] = m_ref[0, 3 * H : 4 * H, :]
    a_ref[H:B, H:] = m_ref[0, 4 * H :, :]
    a_ref[B:, :] = panel_ref[...] * meta[5].astype(F32)
    low = f0_ref[B : 2 * B, :]
    a_ref[...] = a_ref[...] - mul_t(f0_ref[B:, :], low)
    tall_factor(a_ref, f1_ref, dinv_ref, d_ref)
    row = meta[4]

    @pl.when(row == 0)
    def _():
        factor_ref[:, :B] = f0_ref[:B, :]
        factor_ref[:, B:] = jnp.zeros((B, B), F32)

    @pl.when(row == 1)
    def _():
        factor_ref[:, :B] = f0_ref[B : 2 * B, :]
        factor_ref[:, B:] = f1_ref[:B, :]

    @pl.when(row > 1)
    def _():
        factor_ref[:, :B] = f0_ref[2 * B :, :]
        factor_ref[:, B:] = f1_ref[B:, :]


def kernel_c(meta, own_ref, other_ref, f0_ref, f1_ref, d0_ref, d1_ref, factor_ref, window_ref, out_ref, s_ref):
    mine = meta[2]
    live = meta[6].astype(F32)
    for j in range(NX * NZ):
        s_ref[pl.ds(pl.multiple_of((2 * j + mine) * 8, 8), 8), :] = own_ref[j] * live
        s_ref[pl.ds(pl.multiple_of((2 * j + 1 - mine) * 8, 8), 8), :] = other_ref[j] * live
    for k in range(4):
        o, e = k * NB, k * NB + NB
        X = mul_t(s_ref[:, o:e], d0_ref[k])
        s_ref[:, o:e] = X
        s_ref[:, e:] = s_ref[:, e:] - mul_t(X, f0_ref[e : 2 * B, o:e])
    for k in range(4):
        o, e = k * NB, k * NB + NB
        X = mul_t(s_ref[:, B + o : B + e], d1_ref[k])
        s_ref[:, B + o : B + e] = X
        if e < B:
            s_ref[:, B + e :] = s_ref[:, B + e :] - mul_t(X, f1_ref[e:B, o:e])
    out_ref[...] = window_ref[...] - mul_t(factor_ref[...], s_ref[...])


SMEM = pl.BlockSpec(memory_space=pltpu.SMEM)
VM = pl.BlockSpec(memory_space=pltpu.VMEM)


def call(kernel, flops, outs, scratch, *args):
    return pl.pallas_call(
        kernel,
        out_shape=[jax.ShapeDtypeStruct(s, F32) for s in outs],
        in_specs=[SMEM] + [VM] * (len(args) - 1),
        out_specs=[VM] * len(outs),
        scratch_shapes=[pltpu.VMEM(s, F32) for s in scratch],
        compiler_params=pltpu.CompilerParams(vmem_limit_bytes=VMEM_LIMIT),
        cost_estimate=pl.CostEstimate(flops=flops, transcendentals=0, bytes_accessed=8 << 20),
    )(*args)


def rid(x, z, c):
    return (x * NZ + z) * 2 + c


def move(v, keep, to):
    pairs = [
        (rid(x, z, c), rid(*to(x, z, c)))
        for x in range(NX)
        for z in range(NZ)
        for c in range(2)
        if keep(x, z, c)
    ]
    return lax.ppermute(v, "rows", pairs)


def always(x, z, c):
    return True


def by_x(v, d, keep=always):
    return move(v, keep, lambda x, z, c: ((x + d) % NX, z, c))


def by_z(v, d, keep=always):
    return move(v, keep, lambda x, z, c: (x, (z + d) % NZ, c))


def swap_core(v):
    return move(v, always, lambda x, z, c: (x, z, 1 - c))


GROUPS = [[rid(x, z, c) for x in range(NX) for z in range(NZ)] for c in range(2)]


def spread_static(v, x, z, y):
    piece = lax.dynamic_slice_in_dim(v, y * (v.shape[0] // NY), v.shape[0] // NY, 0)
    piece = jnp.where((x == 0) & (z == 0), piece, 0.0)
    piece = piece + sum(by_x(piece, d, lambda x, z, c: x == 0 and z == 0) for d in range(1, NX))
    piece = piece + sum(by_z(piece, d, lambda x, z, c: z == 0) for d in (2, 4, 6))
    piece = piece + by_z(piece, 1, lambda x, z, c: z % 2 == 0)
    own = jnp.stack([piece] + [lax.ppermute(piece, "cols", [(i, (i + d) % NY) for i in range(NY)]) for d in range(1, NY)])
    return own, swap_core(own)


def after(value, *others):
    return lax.optimization_barrier((value,) + others)[0]


def shards(panel, window_block, row_live, window_rows):
    row = lax.axis_index("rows")
    y = lax.axis_index("cols")
    x, z, core = row // (2 * NZ), (row // 2) % NZ, row % 2
    target = window_rows[y]
    live = jnp.where(row < 2, 1, row_live[row])
    meta = jnp.stack([x, z, core, y, row, live, row_live[target], 0]).astype(jnp.int32)

    width = 2 * B // NY
    mine = lax.dynamic_slice_in_dim(panel, y * width, width, 1).reshape(64, 8, width)
    parts = lax.all_to_all(mine, "rows", 0, 0)

    low = lax.ppermute(panel[H:, B:], "rows", [(1, 0)])
    first = jnp.concatenate([panel[:H, :H], panel[H:, :H], panel[H:, H:B], low[:, :H], low[:, H:]])
    second = jnp.concatenate([panel[:H, :H], panel[:H, H:B], panel[H:, :H], panel[H:, H:B], panel[:H, B : B + H]])
    own, other = spread_static(jnp.where(core == 0, first, second), x, z, y)

    chosen = jnp.stack([lax.dynamic_index_in_dim(parts, window_rows[c], 0, keepdims=False) for c in range(NY)])
    quarters = lax.all_to_all(chosen, "cols", 0, 0)
    shard = jnp.concatenate([quarters[q] for q in range(NY)], axis=1)
    t_own = lax.all_to_all(jnp.broadcast_to(shard, (32,) + shard.shape), "rows", 0, 0, axis_index_groups=GROUPS)

    meta_a = after(meta, shard)
    f0, d0 = call(
        kernel_a, 10**10, [(3 * B, B), (4, NB, NB)], [(2, 5 * H, H), (3 * B, B), (NB, NB)], meta_a, own, other, panel[:, :B]
    )
    t_other = swap_core(after(t_own, f0))
    f1, d1, factor = call(
        kernel_b,
        10**10,
        [(2 * B, B), (4, NB, NB), (B, 2 * B)],
        [(2, 5 * H, H), (2 * B, B), (NB, NB)],
        meta, own, other, panel[:, B:], f0,
    )
    (updated,) = call(
        kernel_c, 10**9, [(B, B)], [(B, 2 * B)], meta, t_own, t_other, f0, f1, d0, d1, factor, window_block
    )
    return factor, updated


def solution(mesh):
    in_specs = (P("rows", None), P("rows", "cols"), P(), P())
    out_specs = (P("rows", None), P("rows", "cols"))
    return jax.shard_map(shards, mesh=mesh, in_specs=in_specs, out_specs=out_specs, check_vma=False)
```

```python
import functools

import jax
import jax.numpy as jnp
from jax import lax
from jax.experimental import pallas as pl
from jax.experimental.pallas import tpu as pltpu
from jax.sharding import PartitionSpec as P

F32 = jnp.float32
B = 512
NB = 128
NX, NZ, NY = 4, 8, 4
VMEM_LIMIT = 56 << 20
CONTRACT = (((1,), (1,)), ((), ()))


def lanes(v, j):
    return jnp.broadcast_to(v[:, j : j + 1], (8, NB))


def sublanes(v, s):
    return jnp.broadcast_to(v[s : s + 1, :], (8, NB))


def factor_block(V):
    sub = lax.broadcasted_iota(jnp.int32, (8, NB), 0)
    lane = lax.broadcasted_iota(jnp.int32, (8, NB), 1)
    groups = NB // 8
    E = [jnp.where(lane == sub + 8 * k, 1.0, 0.0).astype(F32) for k in range(groups)]
    upper, inverse = [], []
    for k in range(groups):
        R = [sublanes(V[k], a) for a in range(8)]
        Q = [sublanes(E[k], a) for a in range(8)]
        s = {(a, b): lanes(R[a], 8 * k + b) for a in range(8) for b in range(a + 1)}
        C = {kk: [lanes(V[kk], 8 * k + b) for b in range(8)] for kk in range(k + 1, groups)}
        for b in range(8):
            inv = lax.rsqrt(s[b, b])
            l = {a: s[a, b] * inv for a in range(b + 1, 8)}
            for a in range(b + 1, 8):
                for c in range(b + 1, a + 1):
                    s[a, c] = s[a, c] - l[a] * l[c]
            R[b] = R[b] * inv
            Q[b] = Q[b] * inv
            for a in range(b + 1, 8):
                R[a] = R[a] - l[a] * R[b]
                Q[a] = Q[a] - l[a] * Q[b]
            for kk in C:
                C[kk][b] = C[kk][b] * inv
                for a in range(b + 1, 8):
                    C[kk][a] = C[kk][a] - C[kk][b] * l[a]
        for kk in C:
            for b in range(8):
                V[kk] = V[kk] - C[kk][b] * R[b]
                E[kk] = E[kk] - C[kk][b] * Q[b]
        u, x = R[0], Q[0]
        for a in range(1, 8):
            u = jnp.where(sub == a, R[a], u)
            x = jnp.where(sub == a, Q[a], x)
        upper.append(jnp.where(lane >= sub + 8 * k, u, 0.0))
        inverse.append(x)
    return upper, inverse


def halves(a):
    hi = a.astype(jnp.bfloat16)
    return hi, (a - hi.astype(F32)).astype(jnp.bfloat16)


def mul_t(a, b):
    ah, al = halves(a)
    bh, bl = halves(b)
    d = functools.partial(lax.dot_general, dimension_numbers=CONTRACT, preferred_element_type=F32)
    return d(ah, bh) + (d(ah, bl) + d(al, bh))


def mirrored(d):
    r = lax.broadcasted_iota(jnp.int32, (NB, NB), 0)
    c = lax.broadcasted_iota(jnp.int32, (NB, NB), 1)
    return jnp.where(r >= c, d, d.T)


def tall_factor(a_ref, f_ref, dinv_ref, d_ref):
    m, n = a_ref.shape
    nb = n // NB
    for k in range(nb):
        o = k * NB
        a_ref[o : o + NB, o : o + NB] = mirrored(a_ref[o : o + NB, o : o + NB])
    d_ref[...] = a_ref[0:NB, 0:NB]

    def body(k, carry):
        V = [d_ref[8 * i : 8 * i + 8, :] for i in range(NB // 8)]
        upper, inverse = factor_block(V)
        low = jnp.concatenate(upper, 0).T
        X = jnp.concatenate(inverse, 0)
        dinv_ref[k] = X

        def branch(kk):
            def run():
                o = NB * kk
                e = o + NB
                f_ref[o:e, o:e] = low
                Lp = mul_t(a_ref[e:, o:e], X)
                f_ref[e:, o:e] = Lp
                if e < n:
                    f_ref[o:e, e:] = jnp.zeros((NB, n - e), F32)
                    T = a_ref[e:, e:] - mul_t(Lp, Lp[: n - e])
                    a_ref[e:, e:] = T
                    d_ref[...] = T[:NB, :NB]
                return 0

            return run

        return lax.switch(k, [branch(kk) for kk in range(nb)]) + carry

    lax.fori_loop(0, nb, body, 0)


def place(meta, own_ref, other_ref, m_ref):
    x, y, mine = meta[0], meta[3], meta[2]
    for dy in range(NY):
        for dx in range(NX):
            row = lax.rem(y - dy + NY, NY) * 64 + lax.rem(x - dx + NX, NX) * 16
            for b in range(5):
                at = pl.ds(pl.multiple_of(row + b * H, 16), 16)
                m_ref[mine, at, :] = own_ref[dy, dx, b * 16 : (b + 1) * 16]
                m_ref[1 - mine, at, :] = other_ref[dy, dx, b * 16 : (b + 1) * 16]


H = B // 2


def kernel_a(meta, own_ref, other_ref, panel_ref, f_ref, dinv_ref, m_ref, a_ref, d_ref):
    place(meta, own_ref, other_ref, m_ref)
    a_ref[:H, :H] = m_ref[0, :H, :]
    a_ref[:H, H:] = jnp.zeros((H, H), F32)
    a_ref[H:B, :H] = m_ref[0, H : 2 * H, :]
    a_ref[H:B, H:] = m_ref[0, 2 * H : 3 * H, :]
    for i in range(2):
        for j in range(2):
            o = (2 * i + j) * H
            a_ref[B + i * H : B + (i + 1) * H, j * H : (j + 1) * H] = m_ref[1, o : o + H, :]
    a_ref[2 * B :, :] = panel_ref[...] * meta[5].astype(F32)
    tall_factor(a_ref, f_ref, dinv_ref, d_ref)


def kernel_b(meta, own_ref, other_ref, panel_ref, f0_ref, f1_ref, dinv_ref, factor_ref, m_ref, a_ref, d_ref):
    place(meta, own_ref, other_ref, m_ref)
    a_ref[:H, :H] = m_ref[1, 4 * H :, :]
    a_ref[:H, H:] = jnp.zeros((H, H), F32)
    a_ref[H:B, :H] = m_ref[0, 3 * H : 4 * H, :]
    a_ref[H:B, H:] = m_ref[0, 4 * H :, :]
    a_ref[B:, :] = panel_ref[...] * meta[5].astype(F32)
    low = f0_ref[B : 2 * B, :]
    a_ref[...] = a_ref[...] - mul_t(f0_ref[B:, :], low)
    tall_factor(a_ref, f1_ref, dinv_ref, d_ref)
    row = meta[4]

    @pl.when(row == 0)
    def _():
        factor_ref[:, :B] = f0_ref[:B, :]
        factor_ref[:, B:] = jnp.zeros((B, B), F32)

    @pl.when(row == 1)
    def _():
        factor_ref[:, :B] = f0_ref[B : 2 * B, :]
        factor_ref[:, B:] = f1_ref[:B, :]

    @pl.when(row > 1)
    def _():
        factor_ref[:, :B] = f0_ref[2 * B :, :]
        factor_ref[:, B:] = f1_ref[B:, :]


def kernel_c(meta, own_ref, other_ref, f0_ref, f1_ref, d0_ref, d1_ref, factor_ref, window_ref, out_ref, s_ref):
    mine = meta[2]
    live = meta[6].astype(F32)
    for j in range(NX * NZ):
        s_ref[pl.ds(pl.multiple_of((2 * j + mine) * 8, 8), 8), :] = own_ref[j] * live
        s_ref[pl.ds(pl.multiple_of((2 * j + 1 - mine) * 8, 8), 8), :] = other_ref[j] * live
    for k in range(4):
        o, e = k * NB, k * NB + NB
        X = mul_t(s_ref[:, o:e], d0_ref[k])
        s_ref[:, o:e] = X
        s_ref[:, e:] = s_ref[:, e:] - mul_t(X, f0_ref[e : 2 * B, o:e])
    for k in range(4):
        o, e = k * NB, k * NB + NB
        X = mul_t(s_ref[:, B + o : B + e], d1_ref[k])
        s_ref[:, B + o : B + e] = X
        if e < B:
            s_ref[:, B + e :] = s_ref[:, B + e :] - mul_t(X, f1_ref[e:B, o:e])
    out_ref[...] = window_ref[...] - mul_t(factor_ref[...], s_ref[...])


SMEM = pl.BlockSpec(memory_space=pltpu.SMEM)
VM = pl.BlockSpec(memory_space=pltpu.VMEM)


def call(kernel, flops, outs, scratch, *args):
    return pl.pallas_call(
        kernel,
        out_shape=[jax.ShapeDtypeStruct(s, F32) for s in outs],
        in_specs=[SMEM] + [VM] * (len(args) - 1),
        out_specs=[VM] * len(outs),
        scratch_shapes=[pltpu.VMEM(s, F32) for s in scratch],
        compiler_params=pltpu.CompilerParams(vmem_limit_bytes=VMEM_LIMIT),
        cost_estimate=pl.CostEstimate(flops=flops, transcendentals=0, bytes_accessed=8 << 20),
    )(*args)


def rid(x, z, c):
    return (x * NZ + z) * 2 + c


def move(v, keep, to):
    pairs = [
        (rid(x, z, c), rid(*to(x, z, c)))
        for x in range(NX)
        for z in range(NZ)
        for c in range(2)
        if keep(x, z, c)
    ]
    return lax.ppermute(v, "rows", pairs)


def always(x, z, c):
    return True


def by_x(v, d, keep=always):
    return move(v, keep, lambda x, z, c: ((x + d) % NX, z, c))


def by_z(v, d, keep=always):
    return move(v, keep, lambda x, z, c: (x, (z + d) % NZ, c))


def swap_core(v):
    return move(v, always, lambda x, z, c: (x, z, 1 - c))


GROUPS = [[rid(x, z, c) for x in range(NX) for z in range(NZ)] for c in range(2)]


def spread_static(v, x, z):
    root = (x == 0) & (z == 0)
    piece = jnp.where(root, v[0], 0.0)
    piece = piece + sum(by_x(v[d], d, lambda x, z, c: x == 0 and z == 0) for d in range(1, NX))
    piece = piece + sum(by_z(piece, d, lambda x, z, c: z == 0) for d in (2, 4, 6))
    piece = piece + by_z(piece, 1, lambda x, z, c: z % 2 == 0)
    return jnp.stack([piece] + [by_x(piece, d) for d in range(1, NX)])


def gather_y(v):
    return jnp.stack([v] + [lax.ppermute(v, "cols", [(i, (i + d) % NY) for i in range(NY)]) for d in range(1, NY)])


def after(value, *others):
    return lax.optimization_barrier((value,) + others)[0]


def shards(panel, window_block, row_live, window_rows):
    row = lax.axis_index("rows")
    y = lax.axis_index("cols")
    x, z, core = row // (2 * NZ), (row // 2) % NZ, row % 2
    target = window_rows[y]
    live = jnp.where(row < 2, 1, row_live[row])
    meta = jnp.stack([x, z, core, y, row, live, row_live[target], 0]).astype(jnp.int32)

    width = 2 * B // NY
    mine = lax.dynamic_slice_in_dim(panel, y * width, width, 1).reshape(64, 8, width)
    parts = lax.all_to_all(mine, "rows", 0, 0)

    def rows_of(i):
        return lax.dynamic_slice_in_dim(panel, i * H + y * 64, 64, 0).reshape(NX, 16, 2 * B)

    top, bot = rows_of(0), rows_of(1)
    low = lax.ppermute(bot[:, :, B:], "rows", [(1, 0)])
    first = [top[:, :, :H], bot[:, :, :H], bot[:, :, H:B], low[:, :, :H], low[:, :, H:]]
    second = [top[:, :, :H], top[:, :, H:B], bot[:, :, :H], bot[:, :, H:B], top[:, :, B : B + H]]
    stack = jnp.concatenate([jnp.where(core == 0, f, s) for f, s in zip(first, second)], axis=1)
    part = spread_static(stack, x, z)
    own = gather_y(part)
    other = swap_core(own)

    parts = after(parts, part)
    chosen = jnp.stack([lax.dynamic_index_in_dim(parts, window_rows[c], 0, keepdims=False) for c in range(NY)])
    quarters = lax.all_to_all(chosen, "cols", 0, 0)
    shard = jnp.concatenate([quarters[q] for q in range(NY)], axis=1)
    t_own = lax.all_to_all(jnp.broadcast_to(shard, (32,) + shard.shape), "rows", 0, 0, axis_index_groups=GROUPS)

    meta_a = after(meta, shard)
    f0, d0 = call(
        kernel_a, 10**10, [(3 * B, B), (4, NB, NB)], [(2, 5 * H, H), (3 * B, B), (NB, NB)], meta_a, own, other, panel[:, :B]
    )
    t_other = swap_core(after(t_own, f0))
    f1, d1, factor = call(
        kernel_b,
        10**10,
        [(2 * B, B), (4, NB, NB), (B, 2 * B)],
        [(2, 5 * H, H), (2 * B, B), (NB, NB)],
        meta, own, other, panel[:, B:], f0,
    )
    (updated,) = call(
        kernel_c, 10**9, [(B, B)], [(B, 2 * B)], meta, t_own, t_other, f0, f1, d0, d1, factor, window_block
    )
    return factor, updated


def solution(mesh):
    in_specs = (P("rows", None), P("rows", "cols"), P(), P())
    out_specs = (P("rows", None), P("rows", "cols"))
    return jax.shard_map(shards, mesh=mesh, in_specs=in_specs, out_specs=out_specs, check_vma=False)
```

```python
import functools

import jax
import jax.numpy as jnp
from jax import lax
from jax.experimental import pallas as pl
from jax.experimental.pallas import tpu as pltpu
from jax.sharding import PartitionSpec as P

F32 = jnp.float32
B = 512
NB = 128
H = B // 2
NX, NZ, NY = 4, 8, 4
VMEM_LIMIT = 56 << 20
CONTRACT = (((1,), (1,)), ((), ()))


def lanes(v, j):
    return jnp.broadcast_to(v[:, j : j + 1], (8, NB))


def sublanes(v, s):
    return jnp.broadcast_to(v[s : s + 1, :], (8, NB))


def factor_block(V):
    V = list(V)
    sub = lax.broadcasted_iota(jnp.int32, (8, NB), 0)
    lane = lax.broadcasted_iota(jnp.int32, (8, NB), 1)
    groups = NB // 8
    E = [jnp.where(lane == sub + 8 * k, 1.0, 0.0).astype(F32) for k in range(groups)]
    upper, inverse = [], []
    block = [lanes(V[0], b) for b in range(8)]
    for k in range(groups):
        near = list(range(k + 1, min(groups, k + 3)))
        far = list(range(k + 3, groups))
        R = [sublanes(V[k], a) for a in range(8)]
        Q = [sublanes(E[k], a) for a in range(8)]
        C = {kk: [lanes(V[kk], 8 * k + b) for b in range(8)] for kk in near}
        ahead = [lanes(V[k + 1], 8 * (k + 1) + b) for b in range(8)] if near else None
        D = {kk: [lanes(V[kk], 8 * k + b) for b in range(8)] for kk in far}
        l, invs = {}, []
        for b in range(8):
            inv = lax.rsqrt(sublanes(block[b], b))
            invs.append(inv)
            col = block[b] * inv
            for a in range(b + 1, 8):
                l[a, b] = sublanes(col, a)
            for c in range(b + 1, 8):
                block[c] = block[c] - col * l[c, b]
            for kk in near:
                C[kk][b] = C[kk][b] * inv
                for a in range(b + 1, 8):
                    C[kk][a] = C[kk][a] - C[kk][b] * l[a, b]
            if near:
                x = C[k + 1][b]
                for c in range(8):
                    ahead[c] = ahead[c] - x * sublanes(x, c)
            R[b] = R[b] * inv
            Q[b] = Q[b] * inv
            for a in range(b + 1, 8):
                R[a] = R[a] - l[a, b] * R[b]
                Q[a] = Q[a] - l[a, b] * Q[b]
            for kk in near:
                V[kk] = V[kk] - C[kk][b] * R[b]
                E[kk] = E[kk] - C[kk][b] * Q[b]
        u, x = R[0], Q[0]
        for a in range(1, 8):
            u = jnp.where(sub == a, R[a], u)
            x = jnp.where(sub == a, Q[a], x)
        upper.append(jnp.where(lane >= sub + 8 * k, u, 0.0))
        inverse.append(x)
        if far:
            W, Y = list(R), list(Q)
            for b in reversed(range(8)):
                W[b] = W[b] * invs[b]
                Y[b] = Y[b] * invs[b]
                for a in range(b):
                    W[a] = W[a] - l[b, a] * W[b]
                    Y[a] = Y[a] - l[b, a] * Y[b]
            for kk in far:
                for b in range(8):
                    V[kk] = V[kk] - D[kk][b] * W[b]
                    E[kk] = E[kk] - D[kk][b] * Y[b]
        block = ahead
    return upper, inverse


def halves(a):
    hi = a.astype(jnp.bfloat16)
    return hi, (a - hi.astype(F32)).astype(jnp.bfloat16)


def mul_t(a, b):
    ah, al = halves(a)
    bh, bl = halves(b)
    d = functools.partial(lax.dot_general, dimension_numbers=CONTRACT, preferred_element_type=F32)
    return d(ah, bh) + (d(ah, bl) + d(al, bh))


def mirrored(d):
    r = lax.broadcasted_iota(jnp.int32, (NB, NB), 0)
    c = lax.broadcasted_iota(jnp.int32, (NB, NB), 1)
    return jnp.where(r >= c, d, d.T)


def tall_factor(a_ref, f_ref, dinv_ref, d_ref):
    m, n = a_ref.shape
    nb = n // NB
    for k in range(nb):
        o = k * NB
        a_ref[o : o + NB, o : o + NB] = mirrored(a_ref[o : o + NB, o : o + NB])
    d_ref[...] = a_ref[0:NB, 0:NB]

    def body(k, carry):
        V = [d_ref[8 * i : 8 * i + 8, :] for i in range(NB // 8)]
        upper, inverse = factor_block(V)
        low = jnp.concatenate(upper, 0).T
        X = jnp.concatenate(inverse, 0)
        dinv_ref[k] = X

        def branch(kk):
            def run():
                o = NB * kk
                e = o + NB
                f_ref[o:e, o:e] = low
                if e < m:
                    Lp = mul_t(a_ref[e:, o:e], X)
                    f_ref[e:, o:e] = Lp
                if e < n:
                    f_ref[o:e, e:] = jnp.zeros((NB, n - e), F32)
                    T = a_ref[e:, e:] - mul_t(Lp, Lp[: n - e])
                    a_ref[e:, e:] = T
                    d_ref[...] = T[:NB, :NB]
                return 0

            return run

        return lax.switch(k, [branch(kk) for kk in range(nb)]) + carry

    lax.fori_loop(0, nb, body, 0)


def coords():
    row = lax.axis_index("rows")
    return row // (2 * NZ), lax.axis_index("cols"), lax.rem(row, 2)


def place(own_ref, other_ref, m_ref):
    x, y, mine = coords()
    for dy in range(NY):
        for dx in range(NX):
            row = lax.rem(y - dy + NY, NY) * 64 + lax.rem(x - dx + NX, NX) * 16
            for b in range(5):
                at = pl.ds(pl.multiple_of(row + b * H, 16), 16)
                m_ref[mine, at, :] = own_ref[dy, dx, b * 16 : (b + 1) * 16]
                m_ref[1 - mine, at, :] = other_ref[dy, dx, b * 16 : (b + 1) * 16]


def kernel_a(own_ref, other_ref, f_ref, dinv_ref, m_ref, a_ref, d_ref):
    place(own_ref, other_ref, m_ref)
    a_ref[:H, :H] = m_ref[0, :H, :]
    a_ref[:H, H:] = jnp.zeros((H, H), F32)
    a_ref[H:B, :H] = m_ref[0, H : 2 * H, :]
    a_ref[H:B, H:] = m_ref[0, 2 * H : 3 * H, :]
    for i in range(2):
        for j in range(2):
            o = (2 * i + j) * H
            a_ref[B + i * H : B + (i + 1) * H, j * H : (j + 1) * H] = m_ref[1, o : o + H, :]
    tall_factor(a_ref, f_ref, dinv_ref, d_ref)


def kernel_b(own_ref, other_ref, f0_ref, f1_ref, dinv_ref, m_ref, a_ref, d_ref):
    place(own_ref, other_ref, m_ref)
    a_ref[:H, :H] = m_ref[1, 4 * H :, :]
    a_ref[:H, H:] = jnp.zeros((H, H), F32)
    a_ref[H:, :H] = m_ref[0, 3 * H : 4 * H, :]
    a_ref[H:, H:] = m_ref[0, 4 * H :, :]
    low = f0_ref[B:, :]
    a_ref[...] = a_ref[...] - mul_t(low, low)
    tall_factor(a_ref, f1_ref, dinv_ref, d_ref)


def pair_inverse(d_ref, j, low):
    x0, x1 = d_ref[j], d_ref[j + 1]
    corner = -mul_t(mul_t(x1, low.T), x0.T)
    top = jnp.concatenate([x0, jnp.zeros((NB, NB), F32)], axis=1)
    return jnp.concatenate([top, jnp.concatenate([corner, x1], axis=1)], axis=0)


def kernel_c(live_ref, rows_ref, own_ref, other_ref, f0_ref, f1_ref, d0_ref, d1_ref, panel_ref, window_ref, factor_ref, out_ref, s_ref):
    row = lax.axis_index("rows")
    _, y, mine = coords()
    live_t = live_ref[rows_ref[y]].astype(F32)
    live = jnp.where(row < 2, 1, live_ref[row]).astype(F32)
    s_ref[:B, :] = panel_ref[...] * live
    for j in range(NX * NZ):
        s_ref[pl.ds(pl.multiple_of(B + (2 * j + mine) * 8, 8), 8), :] = own_ref[j] * live_t
        s_ref[pl.ds(pl.multiple_of(B + (2 * j + 1 - mine) * 8, 8), 8), :] = other_ref[j] * live_t
    for k in range(4):
        o, e = k * H, (k + 1) * H
        f_ref, d_ref, base = (f0_ref, d0_ref, 0) if k < 2 else (f1_ref, d1_ref, B)
        p = o - base
        inv = pair_inverse(d_ref, 2 * (k % 2), f_ref[p + NB : p + H, p : p + NB])
        X = mul_t(s_ref[:, o:e], inv)
        s_ref[:, o:e] = X
        if k < 3:
            s_ref[:, e:] = s_ref[:, e:] - mul_t(X, f_ref[p + H :, p : p + H])

    @pl.when(row == 0)
    def _():
        s_ref[:B, :B] = f0_ref[:B, :]
        s_ref[:B, B:] = jnp.zeros((B, B), F32)

    @pl.when(row == 1)
    def _():
        s_ref[:B, :B] = f0_ref[B:, :]
        s_ref[:B, B:] = f1_ref[...]

    factor_ref[...] = s_ref[:B, :]
    out_ref[...] = window_ref[...] - mul_t(s_ref[:B, :], s_ref[B:, :])


def kernel_pick(rows_ref, parts_ref, out_ref):
    out_ref[...] = parts_ref[...]


SMEM = pl.BlockSpec(memory_space=pltpu.SMEM)
VM = pl.BlockSpec(memory_space=pltpu.VMEM)


def call(kernel, flops, outs, scratch, *args):
    return pl.pallas_call(
        kernel,
        out_shape=[jax.ShapeDtypeStruct(s, F32) for s in outs],
        in_specs=[SMEM if a.dtype == jnp.int32 else VM for a in args],
        out_specs=[VM] * len(outs),
        scratch_shapes=[pltpu.VMEM(s, F32) for s in scratch],
        compiler_params=pltpu.CompilerParams(vmem_limit_bytes=VMEM_LIMIT),
        cost_estimate=pl.CostEstimate(flops=flops, transcendentals=0, bytes_accessed=8 << 20),
    )(*args)


def pick(window_rows, parts):
    block = (1,) + parts.shape[1:]
    return pl.pallas_call(
        kernel_pick,
        out_shape=jax.ShapeDtypeStruct((NY,) + parts.shape[1:], F32),
        grid_spec=pltpu.PrefetchScalarGridSpec(
            num_scalar_prefetch=1,
            grid=(NY,),
            in_specs=[pl.BlockSpec(block, lambda i, rows: (rows[i], 0, 0))],
            out_specs=pl.BlockSpec(block, lambda i, rows: (i, 0, 0)),
        ),
    )(window_rows, parts)


def rid(x, z, c):
    return (x * NZ + z) * 2 + c


def move(v, keep, to):
    pairs = [
        (rid(x, z, c), rid(*to(x, z, c)))
        for x in range(NX)
        for z in range(NZ)
        for c in range(2)
        if keep(x, z, c)
    ]
    return lax.ppermute(v, "rows", pairs)


def always(x, z, c):
    return True


def by_x(v, d, keep=always):
    return move(v, keep, lambda x, z, c: ((x + d) % NX, z, c))


def by_z(v, d, keep=always):
    return move(v, keep, lambda x, z, c: (x, (z + d) % NZ, c))


def swap_core(v):
    return move(v, always, lambda x, z, c: (x, z, 1 - c))


GROUPS = [[rid(x, z, c) for x in range(NX) for z in range(NZ)] for c in range(2)]


def spread_static(v, x, z):
    root = (x == 0) & (z == 0)
    piece = jnp.where(root, v[0], 0.0)
    piece = piece + sum(by_x(v[d], d, lambda x, z, c: x == 0 and z == 0) for d in range(1, NX))
    piece = piece + sum(by_z(piece, d, lambda x, z, c: z == 0) for d in (2, 4, 6))
    piece = piece + by_z(piece, 1, lambda x, z, c: z % 2 == 0)
    return jnp.stack([piece] + [by_x(piece, d) for d in range(1, NX)])


def gather_y(v):
    return jnp.stack([v] + [lax.ppermute(v, "cols", [(i, (i + d) % NY) for i in range(NY)]) for d in range(1, NY)])


def after(value, *others):
    return lax.optimization_barrier((value,) + others)[0]


def shards(panel, window_block, row_live, window_rows):
    row = lax.axis_index("rows")
    y = lax.axis_index("cols")
    x, z, core = row // (2 * NZ), (row // 2) % NZ, row % 2
    width = 2 * B // NY
    mine = lax.dynamic_slice_in_dim(panel, y * width, width, 1).reshape(64, 8, width)
    parts = lax.all_to_all(mine, "rows", 0, 0)

    def rows_of(i):
        return lax.dynamic_slice_in_dim(panel, i * H + y * 64, 64, 0).reshape(NX, 16, 2 * B)

    top, bot = rows_of(0), rows_of(1)
    low = lax.ppermute(bot[:, :, B:], "rows", [(1, 0)])
    first = [top[:, :, :H], bot[:, :, :H], bot[:, :, H:B], low[:, :, :H], low[:, :, H:]]
    second = [top[:, :, :H], top[:, :, H:B], bot[:, :, :H], bot[:, :, H:B], top[:, :, B : B + H]]
    stack = jnp.concatenate([jnp.where(core == 0, f, s) for f, s in zip(first, second)], axis=1)
    part = spread_static(stack, x, z)
    own = gather_y(part)
    other = swap_core(own)

    parts = after(parts, part)
    chosen = pick(window_rows, parts)
    quarters = lax.all_to_all(chosen, "cols", 0, 0)
    shard = jnp.concatenate([quarters[q] for q in range(NY)], axis=1)
    t_own = lax.all_to_all(jnp.broadcast_to(shard, (32,) + shard.shape), "rows", 0, 0, axis_index_groups=GROUPS)

    own = after(own, shard)
    f0, d0 = call(kernel_a, 10**10, [(2 * B, B), (4, NB, NB)], [(2, 5 * H, H), (2 * B, B), (NB, NB)], own, other)
    t_other = swap_core(after(t_own, f0))
    f1, d1 = call(kernel_b, 10**10, [(B, B), (4, NB, NB)], [(2, 5 * H, H), (B, B), (NB, NB)], own, other, f0)
    return call(
        kernel_c, 10**9, [(B, 2 * B), (B, B)], [(2 * B, 2 * B)],
        row_live, window_rows, t_own, t_other, f0, f1, d0, d1, panel, window_block,
    )


def solution(mesh):
    in_specs = (P("rows", None), P("rows", "cols"), P(), P())
    out_specs = (P("rows", None), P("rows", "cols"))
    return jax.shard_map(shards, mesh=mesh, in_specs=in_specs, out_specs=out_specs, check_vma=False)
```

```python
import functools

import jax
import jax.numpy as jnp
from jax import lax
from jax.experimental import pallas as pl
from jax.experimental.pallas import tpu as pltpu
from jax.sharding import PartitionSpec as P

F32 = jnp.float32
B = 512
NB = 128
H = B // 2
NX, NZ, NY = 4, 8, 4
CONTRACT = (((1,), (1,)), ((), ()))


def lanes(v, j):
    return jnp.broadcast_to(v[:, j : j + 1], (8, NB))


def sublanes(v, s):
    return jnp.broadcast_to(v[s : s + 1, :], (8, NB))


def factor_block(V):
    V = list(V)
    sub = lax.broadcasted_iota(jnp.int32, (8, NB), 0)
    lane = lax.broadcasted_iota(jnp.int32, (8, NB), 1)
    groups = NB // 8
    E = [jnp.where(lane == sub + 8 * k, 1.0, 0.0).astype(F32) for k in range(groups)]
    upper, inverse = [], []
    block = [lanes(V[0], b) for b in range(8)]
    for k in range(groups):
        near = list(range(k + 1, min(groups, k + 3)))
        far = list(range(k + 3, groups))
        R = [sublanes(V[k], a) for a in range(8)]
        Q = [sublanes(E[k], a) for a in range(8)]
        C = {kk: [lanes(V[kk], 8 * k + b) for b in range(8)] for kk in near}
        ahead = [lanes(V[k + 1], 8 * (k + 1) + b) for b in range(8)] if near else None
        D = {kk: [lanes(V[kk], 8 * k + b) for b in range(8)] for kk in far}
        l, invs = {}, []
        for b in range(8):
            inv = lax.rsqrt(sublanes(block[b], b))
            invs.append(inv)
            col = block[b] * inv
            for a in range(b + 1, 8):
                l[a, b] = sublanes(col, a)
            for c in range(b + 1, 8):
                block[c] = block[c] - col * l[c, b]
            for kk in near:
                C[kk][b] = C[kk][b] * inv
                for a in range(b + 1, 8):
                    C[kk][a] = C[kk][a] - C[kk][b] * l[a, b]
            if near:
                x = C[k + 1][b]
                for c in range(8):
                    ahead[c] = ahead[c] - x * sublanes(x, c)
            R[b] = R[b] * inv
            Q[b] = Q[b] * inv
            for a in range(b + 1, 8):
                R[a] = R[a] - l[a, b] * R[b]
                Q[a] = Q[a] - l[a, b] * Q[b]
            for kk in near:
                V[kk] = V[kk] - C[kk][b] * R[b]
                E[kk] = E[kk] - C[kk][b] * Q[b]
        u, x = R[0], Q[0]
        for a in range(1, 8):
            u = jnp.where(sub == a, R[a], u)
            x = jnp.where(sub == a, Q[a], x)
        upper.append(jnp.where(lane >= sub + 8 * k, u, 0.0))
        inverse.append(x)
        if far:
            W, Y = list(R), list(Q)
            for b in reversed(range(8)):
                W[b] = W[b] * invs[b]
                Y[b] = Y[b] * invs[b]
                for a in range(b):
                    W[a] = W[a] - l[b, a] * W[b]
                    Y[a] = Y[a] - l[b, a] * Y[b]
            for kk in far:
                for b in range(8):
                    V[kk] = V[kk] - D[kk][b] * W[b]
                    E[kk] = E[kk] - D[kk][b] * Y[b]
        block = ahead
    return upper, inverse


def halves(a):
    hi = a.astype(jnp.bfloat16)
    return hi, (a - hi.astype(F32)).astype(jnp.bfloat16)


def mul_t(a, b):
    ah, al = halves(a)
    bh, bl = halves(b)
    d = functools.partial(lax.dot_general, dimension_numbers=CONTRACT, preferred_element_type=F32)
    return d(ah, bh) + (d(ah, bl) + d(al, bh))


def mirrored(d):
    r = lax.broadcasted_iota(jnp.int32, (NB, NB), 0)
    c = lax.broadcasted_iota(jnp.int32, (NB, NB), 1)
    return jnp.where(r >= c, d, d.T)


def tall_factor(a_ref, f_ref, dinv_ref, d_ref):
    m, n = a_ref.shape
    nb = n // NB
    for k in range(nb):
        o = k * NB
        a_ref[o : o + NB, o : o + NB] = mirrored(a_ref[o : o + NB, o : o + NB])
    d_ref[...] = a_ref[0:NB, 0:NB]

    def body(k, carry):
        V = [d_ref[8 * i : 8 * i + 8, :] for i in range(NB // 8)]
        upper, inverse = factor_block(V)
        low = jnp.concatenate(upper, 0).T
        X = jnp.concatenate(inverse, 0)
        dinv_ref[k] = X

        def branch(kk):
            def run():
                o = NB * kk
                e = o + NB
                f_ref[o:e, o:e] = low
                if e < m:
                    Lp = mul_t(a_ref[e:, o:e], X)
                    f_ref[e:, o:e] = Lp
                if e < n:
                    f_ref[o:e, e:] = jnp.zeros((NB, n - e), F32)
                    T = a_ref[e:, e:] - mul_t(Lp, Lp[: n - e])
                    a_ref[e:, e:] = T
                    d_ref[...] = T[:NB, :NB]
                return 0

            return run

        return lax.switch(k, [branch(kk) for kk in range(nb)]) + carry

    lax.fori_loop(0, nb, body, 0)


def coords():
    row = lax.axis_index("rows")
    return row // (2 * NZ), lax.axis_index("cols"), lax.rem(row, 2)


def place(own_ref, other_ref, m_ref):
    x, y, mine = coords()
    for dy in range(NY):
        for dx in range(NX):
            row = lax.rem(y - dy + NY, NY) * 64 + lax.rem(x - dx + NX, NX) * 16
            for b in range(5):
                at = pl.ds(pl.multiple_of(row + b * H, 16), 16)
                m_ref[mine, at, :] = own_ref[dy, dx, b * 16 : (b + 1) * 16]
                m_ref[1 - mine, at, :] = other_ref[dy, dx, b * 16 : (b + 1) * 16]


def kernel_a(own_ref, other_ref, f_ref, dinv_ref, m_ref, a_ref, d_ref):
    place(own_ref, other_ref, m_ref)
    a_ref[:H, :H] = m_ref[0, :H, :]
    a_ref[:H, H:] = jnp.zeros((H, H), F32)
    a_ref[H:B, :H] = m_ref[0, H : 2 * H, :]
    a_ref[H:B, H:] = m_ref[0, 2 * H : 3 * H, :]
    for i in range(2):
        for j in range(2):
            o = (2 * i + j) * H
            a_ref[B + i * H : B + (i + 1) * H, j * H : (j + 1) * H] = m_ref[1, o : o + H, :]
    tall_factor(a_ref, f_ref, dinv_ref, d_ref)


def kernel_b(own_ref, other_ref, f0_ref, f1_ref, dinv_ref, m_ref, a_ref, d_ref):
    place(own_ref, other_ref, m_ref)
    a_ref[:H, :H] = m_ref[1, 4 * H :, :]
    a_ref[:H, H:] = jnp.zeros((H, H), F32)
    a_ref[H:, :H] = m_ref[0, 3 * H : 4 * H, :]
    a_ref[H:, H:] = m_ref[0, 4 * H :, :]
    low = f0_ref[B:, :]
    a_ref[...] = a_ref[...] - mul_t(low, low)
    tall_factor(a_ref, f1_ref, dinv_ref, d_ref)


def pair_inverse(d_ref, j, low):
    x0, x1 = d_ref[j], d_ref[j + 1]
    corner = -mul_t(mul_t(x1, low.T), x0.T)
    top = jnp.concatenate([x0, jnp.zeros((NB, NB), F32)], axis=1)
    return jnp.concatenate([top, jnp.concatenate([corner, x1], axis=1)], axis=0)


def solve_rows(s_ref, inv, f0_ref, f1_ref):
    for k in range(4):
        o, e = k * H, (k + 1) * H
        f_ref, p = (f0_ref, o) if k < 2 else (f1_ref, o - B)
        X = mul_t(s_ref[:, o:e], inv(k))
        s_ref[:, o:e] = X
        if k < 3:
            s_ref[:, e:] = s_ref[:, e:] - mul_t(X, f_ref[p + H :, p : p + H])


def kernel_own(live_ref, f0_ref, f1_ref, d0_ref, d1_ref, panel_ref, factor_ref, inv_ref):
    row = lax.axis_index("rows")
    live = jnp.where(row < 2, 1, live_ref[row]).astype(F32)
    factor_ref[...] = panel_ref[...] * live
    for k in range(4):
        f_ref, d_ref, p = (f0_ref, d0_ref, k * H) if k < 2 else (f1_ref, d1_ref, k * H - B)
        inv_ref[k] = pair_inverse(d_ref, 2 * (k % 2), f_ref[p + NB : p + H, p : p + NB])
    solve_rows(factor_ref, lambda k: inv_ref[k], f0_ref, f1_ref)

    @pl.when(row == 0)
    def _():
        factor_ref[:, :B] = f0_ref[:B, :]
        factor_ref[:, B:] = jnp.zeros((B, B), F32)

    @pl.when(row == 1)
    def _():
        factor_ref[:, :B] = f0_ref[B:, :]
        factor_ref[:, B:] = f1_ref[...]


def kernel_window(live_ref, rows_ref, own_ref, other_ref, f0_ref, f1_ref, inv_ref, factor_ref, window_ref, out_ref, s_ref):
    _, y, mine = coords()
    live_t = live_ref[rows_ref[y]].astype(F32)
    for j in range(NX * NZ):
        s_ref[pl.ds(pl.multiple_of((2 * j + mine) * 8, 8), 8), :] = own_ref[j] * live_t
        s_ref[pl.ds(pl.multiple_of((2 * j + 1 - mine) * 8, 8), 8), :] = other_ref[j] * live_t
    solve_rows(s_ref, lambda k: inv_ref[k], f0_ref, f1_ref)
    out_ref[...] = window_ref[...] - mul_t(factor_ref[...], s_ref[...])


def kernel_pick(rows_ref, parts_ref, out_ref):
    out_ref[...] = parts_ref[...]


SMEM = pl.BlockSpec(memory_space=pltpu.SMEM)
VM = pl.BlockSpec(memory_space=pltpu.VMEM)


def call(kernel, flops, vmem, outs, scratch, *args):
    return pl.pallas_call(
        kernel,
        out_shape=[jax.ShapeDtypeStruct(s, F32) for s in outs],
        in_specs=[SMEM if a.dtype == jnp.int32 else VM for a in args],
        out_specs=[VM] * len(outs),
        scratch_shapes=[pltpu.VMEM(s, F32) for s in scratch],
        compiler_params=pltpu.CompilerParams(vmem_limit_bytes=vmem << 20),
        cost_estimate=pl.CostEstimate(flops=flops, transcendentals=0, bytes_accessed=8 << 20),
    )(*args)


def pick(window_rows, parts):
    block = (1,) + parts.shape[1:]
    return pl.pallas_call(
        kernel_pick,
        out_shape=jax.ShapeDtypeStruct((NY,) + parts.shape[1:], F32),
        grid_spec=pltpu.PrefetchScalarGridSpec(
            num_scalar_prefetch=1,
            grid=(NY,),
            in_specs=[pl.BlockSpec(block, lambda i, rows: (rows[i], 0, 0))],
            out_specs=pl.BlockSpec(block, lambda i, rows: (i, 0, 0)),
        ),
    )(window_rows, parts)


def rid(x, z, c):
    return (x * NZ + z) * 2 + c


def move(v, keep, to):
    pairs = [
        (rid(x, z, c), rid(*to(x, z, c)))
        for x in range(NX)
        for z in range(NZ)
        for c in range(2)
        if keep(x, z, c)
    ]
    return lax.ppermute(v, "rows", pairs)


def always(x, z, c):
    return True


def by_x(v, d, keep=always):
    return move(v, keep, lambda x, z, c: ((x + d) % NX, z, c))


def by_z(v, d, keep=always):
    return move(v, keep, lambda x, z, c: (x, (z + d) % NZ, c))


def swap_core(v):
    return move(v, always, lambda x, z, c: (x, z, 1 - c))


GROUPS = [[rid(x, z, c) for x in range(NX) for z in range(NZ)] for c in range(2)]


def spread_static(v, x, z):
    root = (x == 0) & (z == 0)
    piece = jnp.where(root, v[0], 0.0)
    piece = piece + sum(by_x(v[d], d, lambda x, z, c: x == 0 and z == 0) for d in range(1, NX))
    piece = piece + sum(by_z(piece, d, lambda x, z, c: z == 0) for d in (2, 4, 6))
    piece = piece + by_z(piece, 1, lambda x, z, c: z % 2 == 0)
    return piece, jnp.stack([piece] + [by_x(piece, d) for d in range(1, NX)])


def gather_y(v):
    return jnp.stack([v] + [lax.ppermute(v, "cols", [(i, (i + d) % NY) for i in range(NY)]) for d in range(1, NY)])


def after(value, *others):
    return lax.optimization_barrier((value,) + others)[0]


def shards(panel, window_block, row_live, window_rows):
    row = lax.axis_index("rows")
    y = lax.axis_index("cols")
    x, z, core = row // (2 * NZ), (row // 2) % NZ, row % 2
    width = 2 * B // NY
    mine = lax.dynamic_slice_in_dim(panel, y * width, width, 1).reshape(64, 8, width)
    parts = lax.all_to_all(mine, "rows", 0, 0)

    def rows_of(i):
        return lax.dynamic_slice_in_dim(panel, i * H + y * 64, 64, 0).reshape(NX, 16, 2 * B)

    top, bot = rows_of(0), rows_of(1)
    low = lax.ppermute(bot[:, :, B:], "rows", [(1, 0)])
    first = [top[:, :, :H], bot[:, :, :H], bot[:, :, H:B], low[:, :, :H], low[:, :, H:]]
    second = [top[:, :, :H], top[:, :, H:B], bot[:, :, :H], bot[:, :, H:B], top[:, :, B : B + H]]
    stack = jnp.concatenate([jnp.where(core == 0, f, s) for f, s in zip(first, second)], axis=1)
    piece, part = spread_static(stack, x, z)

    parts = after(parts, piece)
    chosen = pick(window_rows, parts)
    quarters = lax.all_to_all(chosen, "cols", 0, 0)
    shard = jnp.concatenate([quarters[q] for q in range(NY)], axis=1)
    own = gather_y(after(part, shard))
    other = swap_core(own)
    t_own = lax.all_to_all(jnp.broadcast_to(after(shard, part), (32,) + shard.shape), "rows", 0, 0, axis_index_groups=GROUPS)

    f0, d0 = call(kernel_a, 25 * 10**8, 24, [(2 * B, B), (4, NB, NB)], [(2, 5 * H, H), (2 * B, B), (NB, NB)], own, other)
    f1, d1 = call(kernel_b, 25 * 10**8, 20, [(B, B), (4, NB, NB)], [(2, 5 * H, H), (B, B), (NB, NB)], own, other, f0)
    t_other = swap_core(after(t_own, f1))
    factor, inv = call(
        kernel_own, 10**8, 28, [(B, 2 * B), (4, H, H)], [], row_live, f0, f1, d0, d1, panel
    )
    (updated,) = call(
        kernel_window, 10**9, 32, [(B, B)], [(B, 2 * B)],
        row_live, window_rows, t_own, t_other, f0, f1, inv, factor, window_block,
    )
    return factor, updated


def solution(mesh):
    in_specs = (P("rows", None), P("rows", "cols"), P(), P())
    out_specs = (P("rows", None), P("rows", "cols"))
    return jax.shard_map(shards, mesh=mesh, in_specs=in_specs, out_specs=out_specs, check_vma=False)
```

```python
import functools

import jax
import jax.numpy as jnp
from jax import lax
from jax.experimental import pallas as pl
from jax.experimental.pallas import tpu as pltpu
from jax.sharding import PartitionSpec as P

F32 = jnp.float32
B = 512
NB = 128
H = B // 2
NX, NZ, NY = 4, 8, 4
CONTRACT = (((1,), (1,)), ((), ()))


def lanes(v, j):
    return jnp.broadcast_to(v[:, j : j + 1], (8, NB))


def sublanes(v, s):
    return jnp.broadcast_to(v[s : s + 1, :], (8, NB))


def factor_block(V):
    V = list(V)
    sub = lax.broadcasted_iota(jnp.int32, (8, NB), 0)
    lane = lax.broadcasted_iota(jnp.int32, (8, NB), 1)
    groups = NB // 8
    E = [jnp.where(lane == sub + 8 * k, 1.0, 0.0).astype(F32) for k in range(groups)]
    upper, inverse = [], []
    block = [lanes(V[0], b) for b in range(8)]
    for k in range(groups):
        near = list(range(k + 1, min(groups, k + 3)))
        far = list(range(k + 3, groups))
        R = [sublanes(V[k], a) for a in range(8)]
        Q = [sublanes(E[k], a) for a in range(8)]
        C = {kk: [lanes(V[kk], 8 * k + b) for b in range(8)] for kk in near}
        ahead = [lanes(V[k + 1], 8 * (k + 1) + b) for b in range(8)] if near else None
        D = {kk: [lanes(V[kk], 8 * k + b) for b in range(8)] for kk in far}
        l, invs = {}, []
        for b in range(8):
            inv = lax.rsqrt(sublanes(block[b], b))
            invs.append(inv)
            col = block[b] * inv
            for a in range(b + 1, 8):
                l[a, b] = sublanes(col, a)
            for c in range(b + 1, 8):
                block[c] = block[c] - col * l[c, b]
            for kk in near:
                C[kk][b] = C[kk][b] * inv
                for a in range(b + 1, 8):
                    C[kk][a] = C[kk][a] - C[kk][b] * l[a, b]
            if near:
                x = C[k + 1][b]
                for c in range(8):
                    ahead[c] = ahead[c] - x * sublanes(x, c)
            R[b] = R[b] * inv
            Q[b] = Q[b] * inv
            for a in range(b + 1, 8):
                R[a] = R[a] - l[a, b] * R[b]
                Q[a] = Q[a] - l[a, b] * Q[b]
            for kk in near:
                V[kk] = V[kk] - C[kk][b] * R[b]
                E[kk] = E[kk] - C[kk][b] * Q[b]
        u, x = R[0], Q[0]
        for a in range(1, 8):
            u = jnp.where(sub == a, R[a], u)
            x = jnp.where(sub == a, Q[a], x)
        upper.append(jnp.where(lane >= sub + 8 * k, u, 0.0))
        inverse.append(x)
        if far:
            W, Y = list(R), list(Q)
            for b in reversed(range(8)):
                W[b] = W[b] * invs[b]
                Y[b] = Y[b] * invs[b]
                for a in range(b):
                    W[a] = W[a] - l[b, a] * W[b]
                    Y[a] = Y[a] - l[b, a] * Y[b]
            for kk in far:
                for b in range(8):
                    V[kk] = V[kk] - D[kk][b] * W[b]
                    E[kk] = E[kk] - D[kk][b] * Y[b]
        block = ahead
    return upper, inverse


def halves(a):
    hi = a.astype(jnp.bfloat16)
    return hi, (a - hi.astype(F32)).astype(jnp.bfloat16)


def mul_t(a, b):
    ah, al = halves(a)
    bh, bl = halves(b)
    d = functools.partial(lax.dot_general, dimension_numbers=CONTRACT, preferred_element_type=F32)
    return d(ah, bh) + (d(ah, bl) + d(al, bh))


def mirrored(d):
    r = lax.broadcasted_iota(jnp.int32, (NB, NB), 0)
    c = lax.broadcasted_iota(jnp.int32, (NB, NB), 1)
    return jnp.where(r >= c, d, d.T)


def tall_factor(a_ref, f_ref, dinv_ref, d_ref):
    m, n = a_ref.shape
    nb = n // NB
    for k in range(nb):
        o = k * NB
        a_ref[o : o + NB, o : o + NB] = mirrored(a_ref[o : o + NB, o : o + NB])
    d_ref[...] = a_ref[0:NB, 0:NB]

    def body(k, carry):
        V = [d_ref[8 * i : 8 * i + 8, :] for i in range(NB // 8)]
        upper, inverse = factor_block(V)
        low = jnp.concatenate(upper, 0).T
        X = jnp.concatenate(inverse, 0)
        dinv_ref[k] = X

        def branch(kk):
            def run():
                o = NB * kk
                e = o + NB
                f_ref[o:e, o:e] = low
                if e < m:
                    Lp = mul_t(a_ref[e:, o:e], X)
                    f_ref[e:, o:e] = Lp
                if e < n:
                    f_ref[o:e, e:] = jnp.zeros((NB, n - e), F32)
                    T = a_ref[e:, e:] - mul_t(Lp, Lp[: n - e])
                    a_ref[e:, e:] = T
                    d_ref[...] = T[:NB, :NB]
                return 0

            return run

        return lax.switch(k, [branch(kk) for kk in range(nb)]) + carry

    lax.fori_loop(0, nb, body, 0)


def coords():
    row = lax.axis_index("rows")
    return row // (2 * NZ), lax.axis_index("cols"), lax.rem(row, 2)


def place(own_ref, other_ref, m_ref):
    x, y, mine = coords()
    for dy in range(NY):
        for dx in range(NX):
            row = lax.rem(y - dy + NY, NY) * 64 + lax.rem(x - dx + NX, NX) * 16
            for b in range(5):
                at = pl.ds(pl.multiple_of(row + b * H, 16), 16)
                m_ref[mine, at, :] = own_ref[dy, dx, b * 16 : (b + 1) * 16]
                m_ref[1 - mine, at, :] = other_ref[dy, dx, b * 16 : (b + 1) * 16]


def kernel_a(own_ref, other_ref, f_ref, dinv_ref, m_ref, a_ref, d_ref):
    place(own_ref, other_ref, m_ref)
    a_ref[:H, :H] = m_ref[0, :H, :]
    a_ref[:H, H:] = jnp.zeros((H, H), F32)
    a_ref[H:B, :H] = m_ref[0, H : 2 * H, :]
    a_ref[H:B, H:] = m_ref[0, 2 * H : 3 * H, :]
    for i in range(2):
        for j in range(2):
            o = (2 * i + j) * H
            a_ref[B + i * H : B + (i + 1) * H, j * H : (j + 1) * H] = m_ref[1, o : o + H, :]
    tall_factor(a_ref, f_ref, dinv_ref, d_ref)


def kernel_b(own_ref, other_ref, f0_ref, f1_ref, dinv_ref, m_ref, a_ref, d_ref):
    place(own_ref, other_ref, m_ref)
    a_ref[:H, :H] = m_ref[1, 4 * H :, :]
    a_ref[:H, H:] = jnp.zeros((H, H), F32)
    a_ref[H:, :H] = m_ref[0, 3 * H : 4 * H, :]
    a_ref[H:, H:] = m_ref[0, 4 * H :, :]
    low = f0_ref[B:, :]
    a_ref[...] = a_ref[...] - mul_t(low, low)
    tall_factor(a_ref, f1_ref, dinv_ref, d_ref)


def pair_inverse(d_ref, j, low):
    x0, x1 = d_ref[j], d_ref[j + 1]
    corner = -mul_t(mul_t(x1, low.T), x0.T)
    top = jnp.concatenate([x0, jnp.zeros((NB, NB), F32)], axis=1)
    return jnp.concatenate([top, jnp.concatenate([corner, x1], axis=1)], axis=0)


def solve_rows(s_ref, inv, f0_ref, f1_ref):
    for k in range(4):
        o, e = k * H, (k + 1) * H
        f_ref, p = (f0_ref, o) if k < 2 else (f1_ref, o - B)
        X = mul_t(s_ref[:, o:e], inv(k))
        s_ref[:, o:e] = X
        if k < 3:
            s_ref[:, e:] = s_ref[:, e:] - mul_t(X, f_ref[p + H :, p : p + H])


def kernel_own(live_ref, f0_ref, f1_ref, d0_ref, d1_ref, panel_ref, factor_ref, inv_ref):
    row = lax.axis_index("rows")
    live = jnp.where(row < 2, 1, live_ref[row]).astype(F32)
    factor_ref[...] = panel_ref[...] * live
    for k in range(4):
        f_ref, d_ref, p = (f0_ref, d0_ref, k * H) if k < 2 else (f1_ref, d1_ref, k * H - B)
        inv_ref[k] = pair_inverse(d_ref, 2 * (k % 2), f_ref[p + NB : p + H, p : p + NB])
    solve_rows(factor_ref, lambda k: inv_ref[k], f0_ref, f1_ref)

    @pl.when(row == 0)
    def _():
        factor_ref[:, :B] = f0_ref[:B, :]
        factor_ref[:, B:] = jnp.zeros((B, B), F32)

    @pl.when(row == 1)
    def _():
        factor_ref[:, :B] = f0_ref[B:, :]
        factor_ref[:, B:] = f1_ref[...]


def kernel_window(live_ref, rows_ref, own_ref, other_ref, f0_ref, f1_ref, inv_ref, factor_ref, window_ref, out_ref, s_ref):
    _, y, mine = coords()
    live_t = live_ref[rows_ref[y]].astype(F32)
    for j in range(NX * NZ):
        s_ref[pl.ds(pl.multiple_of((2 * j + mine) * 8, 8), 8), :] = own_ref[j] * live_t
        s_ref[pl.ds(pl.multiple_of((2 * j + 1 - mine) * 8, 8), 8), :] = other_ref[j] * live_t
    solve_rows(s_ref, lambda k: inv_ref[k], f0_ref, f1_ref)
    out_ref[...] = window_ref[...] - mul_t(factor_ref[...], s_ref[...])


def kernel_pick(rows_ref, parts_ref, out_ref, sems):
    y = lax.axis_index("cols")
    copies = [
        pltpu.make_async_copy(parts_ref.at[rows_ref[lax.rem(y + d, NY)]], out_ref.at[d], sems.at[d]) for d in range(NY)
    ]
    for c in copies:
        c.start()
    for c in copies:
        c.wait()


def kernel_fan(q0_ref, q1_ref, q2_ref, q3_ref, out_ref):
    y = lax.axis_index("cols")
    width = q0_ref.shape[1]
    for d, q_ref in enumerate((q0_ref, q1_ref, q2_ref, q3_ref)):
        at = pl.ds(pl.multiple_of(lax.rem(y - d + NY, NY) * width, width), width)
        value = q_ref[...]
        for j in range(out_ref.shape[0]):
            out_ref[j, :, at] = value


SMEM = pl.BlockSpec(memory_space=pltpu.SMEM)
VM = pl.BlockSpec(memory_space=pltpu.VMEM)


def call(kernel, flops, vmem, outs, scratch, *args):
    return pl.pallas_call(
        kernel,
        out_shape=[jax.ShapeDtypeStruct(s, F32) for s in outs],
        in_specs=[SMEM if a.dtype == jnp.int32 else VM for a in args],
        out_specs=[VM] * len(outs),
        scratch_shapes=[pltpu.VMEM(s, F32) for s in scratch],
        compiler_params=pltpu.CompilerParams(vmem_limit_bytes=vmem << 20),
        cost_estimate=pl.CostEstimate(flops=flops, transcendentals=0, bytes_accessed=8 << 20),
    )(*args)


def pick(window_rows, parts):
    return pl.pallas_call(
        kernel_pick,
        out_shape=jax.ShapeDtypeStruct((NY,) + parts.shape[1:], F32),
        in_specs=[SMEM, pl.BlockSpec(memory_space=pl.ANY)],
        out_specs=VM,
        scratch_shapes=[pltpu.SemaphoreType.DMA((NY,))],
        compiler_params=pltpu.CompilerParams(vmem_limit_bytes=56 << 20),
    )(window_rows, parts)


def rid(x, z, c):
    return (x * NZ + z) * 2 + c


def move(v, keep, to):
    pairs = [
        (rid(x, z, c), rid(*to(x, z, c)))
        for x in range(NX)
        for z in range(NZ)
        for c in range(2)
        if keep(x, z, c)
    ]
    return lax.ppermute(v, "rows", pairs)


def always(x, z, c):
    return True


def by_x(v, d, keep=always):
    return move(v, keep, lambda x, z, c: ((x + d) % NX, z, c))


def by_z(v, d, keep=always):
    return move(v, keep, lambda x, z, c: (x, (z + d) % NZ, c))


def swap_core(v):
    return move(v, always, lambda x, z, c: (x, z, 1 - c))


GROUPS = [[rid(x, z, c) for x in range(NX) for z in range(NZ)] for c in range(2)]


def spread_static(v, x, z):
    root = (x == 0) & (z == 0)
    piece = jnp.where(root, v[0], 0.0)
    piece = piece + sum(by_x(v[d], d, lambda x, z, c: x == 0 and z == 0) for d in range(1, NX))
    piece = piece + sum(by_z(piece, d, lambda x, z, c: z == 0) for d in (2, 4, 6))
    even = piece
    piece = piece + by_z(piece, 1, lambda x, z, c: z % 2 == 0)
    return even, jnp.stack([piece] + [by_x(piece, d) for d in range(1, NX)])


def by_y(v, d):
    return lax.ppermute(v, "cols", [(i, (i + d) % NY) for i in range(NY)])


def gather_y(v):
    return jnp.stack([v] + [by_y(v, d) for d in range(1, NY)])


def after(value, *others):
    return lax.optimization_barrier((value,) + others)[0]


def shards(panel, window_block, row_live, window_rows):
    row = lax.axis_index("rows")
    y = lax.axis_index("cols")
    x, z, core = row // (2 * NZ), (row // 2) % NZ, row % 2
    width = 2 * B // NY
    mine = lax.dynamic_slice_in_dim(panel, y * width, width, 1).reshape(64, 8, width)
    parts = lax.all_to_all(mine, "rows", 0, 0)

    def rows_of(i):
        return lax.dynamic_slice_in_dim(panel, i * H + y * 64, 64, 0).reshape(NX, 16, 2 * B)

    top, bot = rows_of(0), rows_of(1)
    low = lax.ppermute(bot[:, :, B:], "rows", [(1, 0)])
    first = [top[:, :, :H], bot[:, :, :H], bot[:, :, H:B], low[:, :, :H], low[:, :, H:]]
    second = [top[:, :, :H], top[:, :, H:B], bot[:, :, :H], bot[:, :, H:B], top[:, :, B : B + H]]
    stack = jnp.concatenate([jnp.where(core == 0, f, s) for f, s in zip(first, second)], axis=1)
    piece, part = spread_static(stack, x, z)

    chosen = pick(window_rows, after(parts, piece))
    quarters = [chosen[0]] + [by_y(chosen[d], d) for d in range(1, NY)]
    own = gather_y(after(part, *quarters[1:]))
    other = swap_core(own)
    quarters = after(quarters, part)
    (fan,) = call(kernel_fan, 10**6, 8, [(NX * NZ, 8, 2 * B)], [], *quarters)
    t_own = lax.all_to_all(fan, "rows", 0, 0, axis_index_groups=GROUPS)

    f0, d0 = call(kernel_a, 25 * 10**8, 24, [(2 * B, B), (4, NB, NB)], [(2, 5 * H, H), (2 * B, B), (NB, NB)], own, other)
    f1, d1 = call(kernel_b, 25 * 10**8, 20, [(B, B), (4, NB, NB)], [(2, 5 * H, H), (B, B), (NB, NB)], own, other, f0)
    t_other = swap_core(after(t_own, f1))
    factor, inv = call(
        kernel_own, 10**8, 58, [(B, 2 * B), (4, H, H)], [], row_live, f0, f1, d0, d1, panel
    )
    (updated,) = call(
        kernel_window, 10**8, 58, [(B, B)], [(B, 2 * B)],
        row_live, window_rows, t_own, t_other, f0, f1, inv, factor, window_block,
    )
    return factor, updated


def solution(mesh):
    in_specs = (P("rows", None), P("rows", "cols"), P(), P())
    out_specs = (P("rows", None), P("rows", "cols"))
    return jax.shard_map(shards, mesh=mesh, in_specs=in_specs, out_specs=out_specs, check_vma=False)
```

```python
import functools

import jax
import jax.numpy as jnp
from jax import lax
from jax.experimental import pallas as pl
from jax.experimental.pallas import tpu as pltpu
from jax.sharding import PartitionSpec as P

F32 = jnp.float32
B = 512
NB = 128
H = B // 2
COST = 25 * 10**8
NX, NZ, NY = 4, 8, 4
CONTRACT = (((1,), (1,)), ((), ()))


def lanes(v, j):
    return jnp.broadcast_to(v[:, j : j + 1], (8, NB))


def sublanes(v, s):
    return jnp.broadcast_to(v[s : s + 1, :], (8, NB))


def factor_block(V):
    V = list(V)
    sub = lax.broadcasted_iota(jnp.int32, (8, NB), 0)
    lane = lax.broadcasted_iota(jnp.int32, (8, NB), 1)
    groups = NB // 8
    E = [jnp.where(lane == sub + 8 * k, 1.0, 0.0).astype(F32) for k in range(groups)]
    upper, inverse = [], []
    block = [lanes(V[0], b) for b in range(8)]
    for k in range(groups):
        near = list(range(k + 1, min(groups, k + 3)))
        far = list(range(k + 3, groups))
        R = [sublanes(V[k], a) for a in range(8)]
        Q = [sublanes(E[k], a) for a in range(8)]
        C = {kk: [lanes(V[kk], 8 * k + b) for b in range(8)] for kk in near}
        ahead = [lanes(V[k + 1], 8 * (k + 1) + b) for b in range(8)] if near else None
        D = {kk: [lanes(V[kk], 8 * k + b) for b in range(8)] for kk in far}
        l, invs = {}, []
        for b in range(8):
            inv = lax.rsqrt(sublanes(block[b], b))
            invs.append(inv)
            col = block[b] * inv
            for a in range(b + 1, 8):
                l[a, b] = sublanes(col, a)
            for c in range(b + 1, 8):
                block[c] = block[c] - col * l[c, b]
            for kk in near:
                C[kk][b] = C[kk][b] * inv
                for a in range(b + 1, 8):
                    C[kk][a] = C[kk][a] - C[kk][b] * l[a, b]
            if near:
                x = C[k + 1][b]
                for c in range(8):
                    ahead[c] = ahead[c] - x * sublanes(x, c)
            R[b] = R[b] * inv
            Q[b] = Q[b] * inv
            for a in range(b + 1, 8):
                R[a] = R[a] - l[a, b] * R[b]
                Q[a] = Q[a] - l[a, b] * Q[b]
            for kk in near:
                V[kk] = V[kk] - C[kk][b] * R[b]
                E[kk] = E[kk] - C[kk][b] * Q[b]
        u, x = R[0], Q[0]
        for a in range(1, 8):
            u = jnp.where(sub == a, R[a], u)
            x = jnp.where(sub == a, Q[a], x)
        upper.append(jnp.where(lane >= sub + 8 * k, u, 0.0))
        inverse.append(x)
        if far:
            W, Y = list(R), list(Q)
            for b in reversed(range(8)):
                W[b] = W[b] * invs[b]
                Y[b] = Y[b] * invs[b]
                for a in range(b):
                    W[a] = W[a] - l[b, a] * W[b]
                    Y[a] = Y[a] - l[b, a] * Y[b]
            for kk in far:
                for b in range(8):
                    V[kk] = V[kk] - D[kk][b] * W[b]
                    E[kk] = E[kk] - D[kk][b] * Y[b]
        block = ahead
    return upper, inverse


def halves(a):
    hi = a.astype(jnp.bfloat16)
    return hi, (a - hi.astype(F32)).astype(jnp.bfloat16)


def mul_t(a, b):
    ah, al = halves(a)
    bh, bl = halves(b)
    d = functools.partial(lax.dot_general, dimension_numbers=CONTRACT, preferred_element_type=F32)
    return d(ah, bh) + (d(ah, bl) + d(al, bh))


def mirrored(d):
    r = lax.broadcasted_iota(jnp.int32, (NB, NB), 0)
    c = lax.broadcasted_iota(jnp.int32, (NB, NB), 1)
    return jnp.where(r >= c, d, d.T)


def tall_factor(a_ref, f_ref, dinv_ref, d_ref):
    m, n = a_ref.shape
    nb = n // NB
    for k in range(nb):
        o = k * NB
        a_ref[o : o + NB, o : o + NB] = mirrored(a_ref[o : o + NB, o : o + NB])
    d_ref[...] = a_ref[0:NB, 0:NB]

    def body(k, carry):
        V = [d_ref[8 * i : 8 * i + 8, :] for i in range(NB // 8)]
        upper, inverse = factor_block(V)
        low = jnp.concatenate(upper, 0).T
        X = jnp.concatenate(inverse, 0)
        dinv_ref[k] = X

        def branch(kk):
            def run():
                o = NB * kk
                e = o + NB
                f_ref[o:e, o:e] = low
                if e < m:
                    Lp = mul_t(a_ref[e:, o:e], X)
                    f_ref[e:, o:e] = Lp
                if e < n:
                    f_ref[o:e, e:] = jnp.zeros((NB, n - e), F32)
                    T = a_ref[e:, e:] - mul_t(Lp, Lp[: n - e])
                    a_ref[e:, e:] = T
                    d_ref[...] = T[:NB, :NB]
                return 0

            return run

        return lax.switch(k, [branch(kk) for kk in range(nb)]) + carry

    lax.fori_loop(0, nb, body, 0)


def coords():
    row = lax.axis_index("rows")
    return row // (2 * NZ), lax.axis_index("cols"), lax.rem(row, 2)


def place(own_ref, other_ref, m_ref):
    x, y, mine = coords()
    for dy in range(NY):
        for dx in range(NX):
            row = lax.rem(y - dy + NY, NY) * 64 + lax.rem(x - dx + NX, NX) * 16
            for b in range(5):
                at = pl.ds(pl.multiple_of(row + b * H, 16), 16)
                m_ref[mine, at, :] = own_ref[dy, dx, b * 16 : (b + 1) * 16]
                m_ref[1 - mine, at, :] = other_ref[dy, dx, b * 16 : (b + 1) * 16]


def kernel_a(own_ref, other_ref, f_ref, dinv_ref, m_ref, a_ref, d_ref):
    place(own_ref, other_ref, m_ref)
    a_ref[:H, :H] = m_ref[0, :H, :]
    a_ref[:H, H:] = jnp.zeros((H, H), F32)
    a_ref[H:B, :H] = m_ref[0, H : 2 * H, :]
    a_ref[H:B, H:] = m_ref[0, 2 * H : 3 * H, :]
    for i in range(2):
        for j in range(2):
            o = (2 * i + j) * H
            a_ref[B + i * H : B + (i + 1) * H, j * H : (j + 1) * H] = m_ref[1, o : o + H, :]
    tall_factor(a_ref, f_ref, dinv_ref, d_ref)


def kernel_b(own_ref, other_ref, f0_ref, f1_ref, dinv_ref, m_ref, a_ref, d_ref):
    place(own_ref, other_ref, m_ref)
    a_ref[:H, :H] = m_ref[1, 4 * H :, :]
    a_ref[:H, H:] = jnp.zeros((H, H), F32)
    a_ref[H:, :H] = m_ref[0, 3 * H : 4 * H, :]
    a_ref[H:, H:] = m_ref[0, 4 * H :, :]
    low = f0_ref[B:, :]
    a_ref[...] = a_ref[...] - mul_t(low, low)
    tall_factor(a_ref, f1_ref, dinv_ref, d_ref)


def pair_inverse(d_ref, j, low):
    x0, x1 = d_ref[j], d_ref[j + 1]
    corner = -mul_t(mul_t(x1, low.T), x0.T)
    top = jnp.concatenate([x0, jnp.zeros((NB, NB), F32)], axis=1)
    return jnp.concatenate([top, jnp.concatenate([corner, x1], axis=1)], axis=0)


def solve_rows(s_ref, inv, f0_ref, f1_ref):
    for k in range(4):
        o, e = k * H, (k + 1) * H
        f_ref, p = (f0_ref, o) if k < 2 else (f1_ref, o - B)
        X = mul_t(s_ref[:, o:e], inv(k))
        s_ref[:, o:e] = X
        if k < 3:
            s_ref[:, e:] = s_ref[:, e:] - mul_t(X, f_ref[p + H :, p : p + H])


def kernel_c(live_ref, rows_ref, own_ref, other_ref, f0_ref, f1_ref, d0_ref, d1_ref, panel_ref, window_ref, factor_ref, out_ref, s_ref):
    row = lax.axis_index("rows")
    _, y, mine = coords()
    live_t = live_ref[rows_ref[y]].astype(F32)
    live = jnp.where(row < 2, 1, live_ref[row]).astype(F32)
    s_ref[:B, :] = panel_ref[...] * live
    for j in range(NX * NZ):
        s_ref[pl.ds(pl.multiple_of(B + (2 * j + mine) * 8, 8), 8), :] = own_ref[j] * live_t
        s_ref[pl.ds(pl.multiple_of(B + (2 * j + 1 - mine) * 8, 8), 8), :] = other_ref[j] * live_t
    inv = []
    for k in range(4):
        f_ref, d_ref, p = (f0_ref, d0_ref, k * H) if k < 2 else (f1_ref, d1_ref, k * H - B)
        inv.append(pair_inverse(d_ref, 2 * (k % 2), f_ref[p + NB : p + H, p : p + NB]))
    solve_rows(s_ref, lambda k: inv[k], f0_ref, f1_ref)

    @pl.when(row == 0)
    def _():
        s_ref[:B, :B] = f0_ref[:B, :]
        s_ref[:B, B:] = jnp.zeros((B, B), F32)

    @pl.when(row == 1)
    def _():
        s_ref[:B, :B] = f0_ref[B:, :]
        s_ref[:B, B:] = f1_ref[...]

    factor_ref[...] = s_ref[:B, :]
    out_ref[...] = window_ref[...] - mul_t(s_ref[:B, :], s_ref[B:, :])


def kernel_pick(rows_ref, parts_ref, out_ref, sems):
    y = lax.axis_index("cols")
    copies = [
        pltpu.make_async_copy(parts_ref.at[rows_ref[lax.rem(y + d, NY)]], out_ref.at[d], sems.at[d]) for d in range(NY)
    ]
    for c in copies:
        c.start()
    for c in copies:
        c.wait()


def kernel_fan(q0_ref, q1_ref, q2_ref, q3_ref, out_ref):
    y = lax.axis_index("cols")
    width = q0_ref.shape[1]
    for d, q_ref in enumerate((q0_ref, q1_ref, q2_ref, q3_ref)):
        at = pl.ds(pl.multiple_of(lax.rem(y - d + NY, NY) * width, width), width)
        value = q_ref[...]
        for j in range(out_ref.shape[0]):
            out_ref[j, :, at] = value


SMEM = pl.BlockSpec(memory_space=pltpu.SMEM)
VM = pl.BlockSpec(memory_space=pltpu.VMEM)


def call(kernel, flops, vmem, outs, scratch, *args):
    return pl.pallas_call(
        kernel,
        out_shape=[jax.ShapeDtypeStruct(s, F32) for s in outs],
        in_specs=[SMEM if a.dtype == jnp.int32 else VM for a in args],
        out_specs=[VM] * len(outs),
        scratch_shapes=[pltpu.VMEM(s, F32) for s in scratch],
        compiler_params=pltpu.CompilerParams(vmem_limit_bytes=vmem << 20),
        cost_estimate=pl.CostEstimate(flops=flops, transcendentals=0, bytes_accessed=8 << 20),
    )(*args)


def pick(window_rows, parts):
    return pl.pallas_call(
        kernel_pick,
        out_shape=jax.ShapeDtypeStruct((NY,) + parts.shape[1:], F32),
        in_specs=[SMEM, pl.BlockSpec(memory_space=pl.ANY)],
        out_specs=VM,
        scratch_shapes=[pltpu.SemaphoreType.DMA((NY,))],
        compiler_params=pltpu.CompilerParams(vmem_limit_bytes=56 << 20),
    )(window_rows, parts)


def rid(x, z, c):
    return (x * NZ + z) * 2 + c


def move(v, keep, to):
    pairs = [
        (rid(x, z, c), rid(*to(x, z, c)))
        for x in range(NX)
        for z in range(NZ)
        for c in range(2)
        if keep(x, z, c)
    ]
    return lax.ppermute(v, "rows", pairs)


def always(x, z, c):
    return True


def by_x(v, d, keep=always):
    return move(v, keep, lambda x, z, c: ((x + d) % NX, z, c))


def by_z(v, d, keep=always):
    return move(v, keep, lambda x, z, c: (x, (z + d) % NZ, c))


def swap_core(v):
    return move(v, always, lambda x, z, c: (x, z, 1 - c))


GROUPS = [[rid(x, z, c) for x in range(NX) for z in range(NZ)] for c in range(2)]


def spread_static(v, x, z):
    root = (x == 0) & (z == 0)
    piece = jnp.where(root, v[0], 0.0)
    piece = piece + sum(by_x(v[d], d, lambda x, z, c: x == 0 and z == 0) for d in range(1, NX))
    piece = piece + sum(by_z(piece, d, lambda x, z, c: z == 0) for d in (2, 4, 6))
    piece = piece + by_z(piece, 1, lambda x, z, c: z % 2 == 0)
    return piece, jnp.stack([piece] + [by_x(piece, d) for d in range(1, NX)])


def by_y(v, d):
    return lax.ppermute(v, "cols", [(i, (i + d) % NY) for i in range(NY)])


def gather_y(v):
    return jnp.stack([v] + [by_y(v, d) for d in range(1, NY)])


def after(value, *others):
    return lax.optimization_barrier((value,) + others)[0]


def shards(panel, window_block, row_live, window_rows):
    row = lax.axis_index("rows")
    y = lax.axis_index("cols")
    x, z, core = row // (2 * NZ), (row // 2) % NZ, row % 2

    def rows_of(i):
        return lax.dynamic_slice_in_dim(panel, i * H + y * 64, 64, 0).reshape(NX, 16, 2 * B)

    top, bot = rows_of(0), rows_of(1)
    low = lax.ppermute(bot[:, :, B:], "rows", [(1, 0)])
    first = [top[:, :, :H], bot[:, :, :H], bot[:, :, H:B], low[:, :, :H], low[:, :, H:]]
    second = [top[:, :, :H], top[:, :, H:B], bot[:, :, :H], bot[:, :, H:B], top[:, :, B : B + H]]
    stack = jnp.concatenate([jnp.where(core == 0, f, s) for f, s in zip(first, second)], axis=1)
    piece, part = spread_static(stack, x, z)

    width = 2 * B // NY
    mine = lax.dynamic_slice_in_dim(panel, y * width, width, 1).reshape(64, 8, width)
    parts = lax.all_to_all(after(mine, piece), "rows", 0, 0)

    own = gather_y(part)
    other = swap_core(own)
    chosen = pick(window_rows, after(parts, part))
    quarters = [chosen[0]] + [by_y(chosen[d], d) for d in range(1, NY)]
    quarters = after(quarters, own)
    (fan,) = call(kernel_fan, 10**6, 8, [(NX * NZ, 8, 2 * B)], [], *quarters)
    t_own = lax.all_to_all(fan, "rows", 0, 0, axis_index_groups=GROUPS)

    f0, d0 = call(kernel_a, COST, 60, [(2 * B, B), (4, NB, NB)], [(2, 5 * H, H), (2 * B, B), (NB, NB)], own, other)
    f1, d1 = call(kernel_b, COST, 60, [(B, B), (4, NB, NB)], [(2, 5 * H, H), (B, B), (NB, NB)], own, other, f0)
    t_other = swap_core(after(t_own, f1))
    return call(
        kernel_c, 10**8, 60, [(B, 2 * B), (B, B)], [(2 * B, 2 * B)],
        row_live, window_rows, t_own, t_other, f0, f1, d0, d1, panel, window_block,
    )


def solution(mesh):
    in_specs = (P("rows", None), P("rows", "cols"), P(), P())
    out_specs = (P("rows", None), P("rows", "cols"))
    return jax.shard_map(shards, mesh=mesh, in_specs=in_specs, out_specs=out_specs, check_vma=False)
```

```python
import functools

import jax
import jax.numpy as jnp
from jax import lax
from jax.experimental import pallas as pl
from jax.experimental.pallas import tpu as pltpu
from jax.sharding import PartitionSpec as P

F32 = jnp.float32
B = 512
NB = 128
H = B // 2
COST = 35 * 10**8
NX, NZ, NY = 4, 8, 4
CONTRACT = (((1,), (1,)), ((), ()))


def lanes(v, j):
    return jnp.broadcast_to(v[:, j : j + 1], (8, NB))


def sublanes(v, s):
    return jnp.broadcast_to(v[s : s + 1, :], (8, NB))


def factor_block(V):
    V = list(V)
    sub = lax.broadcasted_iota(jnp.int32, (8, NB), 0)
    lane = lax.broadcasted_iota(jnp.int32, (8, NB), 1)
    groups = NB // 8
    E = [jnp.where(lane == sub + 8 * k, 1.0, 0.0).astype(F32) for k in range(groups)]
    upper, inverse = [], []
    block = [lanes(V[0], b) for b in range(8)]
    for k in range(groups):
        near = list(range(k + 1, min(groups, k + 3)))
        far = list(range(k + 3, groups))
        R = [sublanes(V[k], a) for a in range(8)]
        Q = [sublanes(E[k], a) for a in range(8)]
        C = {kk: [lanes(V[kk], 8 * k + b) for b in range(8)] for kk in near}
        ahead = [lanes(V[k + 1], 8 * (k + 1) + b) for b in range(8)] if near else None
        D = {kk: [lanes(V[kk], 8 * k + b) for b in range(8)] for kk in far}
        l, invs = {}, []
        for b in range(8):
            inv = lax.rsqrt(sublanes(block[b], b))
            invs.append(inv)
            col = block[b] * inv
            for a in range(b + 1, 8):
                l[a, b] = sublanes(col, a)
            for c in range(b + 1, 8):
                block[c] = block[c] - col * l[c, b]
            for kk in near:
                C[kk][b] = C[kk][b] * inv
                for a in range(b + 1, 8):
                    C[kk][a] = C[kk][a] - C[kk][b] * l[a, b]
            if near:
                x = C[k + 1][b]
                for c in range(8):
                    ahead[c] = ahead[c] - x * sublanes(x, c)
            R[b] = R[b] * inv
            Q[b] = Q[b] * inv
            for a in range(b + 1, 8):
                R[a] = R[a] - l[a, b] * R[b]
                Q[a] = Q[a] - l[a, b] * Q[b]
            for kk in near:
                V[kk] = V[kk] - C[kk][b] * R[b]
                E[kk] = E[kk] - C[kk][b] * Q[b]
        u, x = R[0], Q[0]
        for a in range(1, 8):
            u = jnp.where(sub == a, R[a], u)
            x = jnp.where(sub == a, Q[a], x)
        upper.append(jnp.where(lane >= sub + 8 * k, u, 0.0))
        inverse.append(x)
        if far:
            W, Y = list(R), list(Q)
            for b in reversed(range(8)):
                W[b] = W[b] * invs[b]
                Y[b] = Y[b] * invs[b]
                for a in range(b):
                    W[a] = W[a] - l[b, a] * W[b]
                    Y[a] = Y[a] - l[b, a] * Y[b]
            for kk in far:
                for b in range(8):
                    V[kk] = V[kk] - D[kk][b] * W[b]
                    E[kk] = E[kk] - D[kk][b] * Y[b]
        block = ahead
    return upper, inverse


def halves(a):
    hi = a.astype(jnp.bfloat16)
    return hi, (a - hi.astype(F32)).astype(jnp.bfloat16)


def mul_t(a, b):
    ah, al = halves(a)
    bh, bl = halves(b)
    d = functools.partial(lax.dot_general, dimension_numbers=CONTRACT, preferred_element_type=F32)
    return d(ah, bh) + (d(ah, bl) + d(al, bh))


def mirrored(d):
    r = lax.broadcasted_iota(jnp.int32, (NB, NB), 0)
    c = lax.broadcasted_iota(jnp.int32, (NB, NB), 1)
    return jnp.where(r >= c, d, d.T)


def tall_factor(a_ref, f_ref, dinv_ref, d_ref):
    m, n = a_ref.shape
    nb = n // NB
    for k in range(nb):
        o = k * NB
        a_ref[o : o + NB, o : o + NB] = mirrored(a_ref[o : o + NB, o : o + NB])
    d_ref[...] = a_ref[0:NB, 0:NB]

    def body(k, carry):
        V = [d_ref[8 * i : 8 * i + 8, :] for i in range(NB // 8)]
        upper, inverse = factor_block(V)
        low = jnp.concatenate(upper, 0).T
        X = jnp.concatenate(inverse, 0)
        dinv_ref[k] = X

        def branch(kk):
            def run():
                o = NB * kk
                e = o + NB
                f_ref[o:e, o:e] = low
                if e < m:
                    Lp = mul_t(a_ref[e:, o:e], X)
                    f_ref[e:, o:e] = Lp
                if e < n:
                    f_ref[o:e, e:] = jnp.zeros((NB, n - e), F32)
                    T = a_ref[e:, e:] - mul_t(Lp, Lp[: n - e])
                    a_ref[e:, e:] = T
                    d_ref[...] = T[:NB, :NB]
                return 0

            return run

        return lax.switch(k, [branch(kk) for kk in range(nb)]) + carry

    lax.fori_loop(0, nb, body, 0)


def coords():
    row = lax.axis_index("rows")
    return row // (2 * NZ), lax.axis_index("cols"), lax.rem(row, 2)


def place(own_ref, other_ref, m_ref):
    x, y, mine = coords()
    for dy in range(NY):
        for dx in range(NX):
            row = lax.rem(y - dy + NY, NY) * 64 + lax.rem(x - dx + NX, NX) * 16
            for b in range(5):
                at = pl.ds(pl.multiple_of(row + b * H, 16), 16)
                m_ref[mine, at, :] = own_ref[dy, dx, b * 16 : (b + 1) * 16]
                m_ref[1 - mine, at, :] = other_ref[dy, dx, b * 16 : (b + 1) * 16]


def kernel_a(own_ref, other_ref, f_ref, dinv_ref, m_ref, a_ref, d_ref):
    place(own_ref, other_ref, m_ref)
    a_ref[:H, :H] = m_ref[0, :H, :]
    a_ref[:H, H:] = jnp.zeros((H, H), F32)
    a_ref[H:B, :H] = m_ref[0, H : 2 * H, :]
    a_ref[H:B, H:] = m_ref[0, 2 * H : 3 * H, :]
    for i in range(2):
        for j in range(2):
            o = (2 * i + j) * H
            a_ref[B + i * H : B + (i + 1) * H, j * H : (j + 1) * H] = m_ref[1, o : o + H, :]
    tall_factor(a_ref, f_ref, dinv_ref, d_ref)


def kernel_b(own_ref, other_ref, f0_ref, f1_ref, dinv_ref, m_ref, a_ref, d_ref):
    place(own_ref, other_ref, m_ref)
    a_ref[:H, :H] = m_ref[1, 4 * H :, :]
    a_ref[:H, H:] = jnp.zeros((H, H), F32)
    a_ref[H:, :H] = m_ref[0, 3 * H : 4 * H, :]
    a_ref[H:, H:] = m_ref[0, 4 * H :, :]
    low = f0_ref[B:, :]
    a_ref[...] = a_ref[...] - mul_t(low, low)
    tall_factor(a_ref, f1_ref, dinv_ref, d_ref)


def pair_inverse(d_ref, j, low):
    x0, x1 = d_ref[j], d_ref[j + 1]
    corner = -mul_t(mul_t(x1, low.T), x0.T)
    top = jnp.concatenate([x0, jnp.zeros((NB, NB), F32)], axis=1)
    return jnp.concatenate([top, jnp.concatenate([corner, x1], axis=1)], axis=0)


def solve_rows(s_ref, inv, f0_ref, f1_ref):
    for k in range(4):
        o, e = k * H, (k + 1) * H
        f_ref, p = (f0_ref, o) if k < 2 else (f1_ref, o - B)
        X = mul_t(s_ref[:, o:e], inv(k))
        s_ref[:, o:e] = X
        if k < 3:
            s_ref[:, e:] = s_ref[:, e:] - mul_t(X, f_ref[p + H :, p : p + H])


def kernel_c(live_ref, rows_ref, own_ref, other_ref, f0_ref, f1_ref, d0_ref, d1_ref, panel_ref, window_ref, factor_ref, out_ref, s_ref):
    row = lax.axis_index("rows")
    _, y, mine = coords()
    live_t = live_ref[rows_ref[y]].astype(F32)
    live = jnp.where(row < 2, 1, live_ref[row]).astype(F32)
    s_ref[:B, :] = panel_ref[...] * live
    for j in range(NX * NZ):
        s_ref[pl.ds(pl.multiple_of(B + (2 * j + mine) * 8, 8), 8), :] = own_ref[j] * live_t
        s_ref[pl.ds(pl.multiple_of(B + (2 * j + 1 - mine) * 8, 8), 8), :] = other_ref[j] * live_t
    inv = []
    for k in range(4):
        f_ref, d_ref, p = (f0_ref, d0_ref, k * H) if k < 2 else (f1_ref, d1_ref, k * H - B)
        inv.append(pair_inverse(d_ref, 2 * (k % 2), f_ref[p + NB : p + H, p : p + NB]))
    solve_rows(s_ref, lambda k: inv[k], f0_ref, f1_ref)

    @pl.when(row == 0)
    def _():
        s_ref[:B, :B] = f0_ref[:B, :]
        s_ref[:B, B:] = jnp.zeros((B, B), F32)

    @pl.when(row == 1)
    def _():
        s_ref[:B, :B] = f0_ref[B:, :]
        s_ref[:B, B:] = f1_ref[...]

    factor_ref[...] = s_ref[:B, :]
    out_ref[...] = window_ref[...] - mul_t(s_ref[:B, :], s_ref[B:, :])


def kernel_pick(rows_ref, parts_ref, *refs):
    y = lax.axis_index("cols")
    outs, sems = refs[:NY], refs[NY]
    copies = [
        pltpu.make_async_copy(parts_ref.at[rows_ref[lax.rem(y + d, NY)]], outs[d], sems.at[d]) for d in range(NY)
    ]
    for c in copies:
        c.start()
    for c in copies:
        c.wait()


def kernel_fan(q0_ref, q1_ref, q2_ref, q3_ref, out_ref):
    y = lax.axis_index("cols")
    width = q0_ref.shape[1]
    for d, q_ref in enumerate((q0_ref, q1_ref, q2_ref, q3_ref)):
        at = pl.ds(pl.multiple_of(lax.rem(y - d + NY, NY) * width, width), width)
        value = q_ref[...]
        for j in range(out_ref.shape[0]):
            out_ref[j, :, at] = value


SMEM = pl.BlockSpec(memory_space=pltpu.SMEM)
VM = pl.BlockSpec(memory_space=pltpu.VMEM)


def call(kernel, flops, vmem, outs, scratch, *args):
    return pl.pallas_call(
        kernel,
        out_shape=[jax.ShapeDtypeStruct(s, F32) for s in outs],
        in_specs=[SMEM if a.dtype == jnp.int32 else VM for a in args],
        out_specs=[VM] * len(outs),
        scratch_shapes=[pltpu.VMEM(s, F32) for s in scratch],
        compiler_params=pltpu.CompilerParams(vmem_limit_bytes=vmem << 20),
        cost_estimate=pl.CostEstimate(flops=flops, transcendentals=0, bytes_accessed=8 << 20),
    )(*args)


def pick(window_rows, parts):
    return pl.pallas_call(
        kernel_pick,
        out_shape=[jax.ShapeDtypeStruct(parts.shape[1:], F32)] * NY,
        in_specs=[SMEM, pl.BlockSpec(memory_space=pltpu.HBM)],
        out_specs=[VM] * NY,
        scratch_shapes=[pltpu.SemaphoreType.DMA((NY,))],
        compiler_params=pltpu.CompilerParams(vmem_limit_bytes=8 << 20),
    )(window_rows, parts)


def rid(x, z, c):
    return (x * NZ + z) * 2 + c


def move(v, keep, to):
    pairs = [
        (rid(x, z, c), rid(*to(x, z, c)))
        for x in range(NX)
        for z in range(NZ)
        for c in range(2)
        if keep(x, z, c)
    ]
    return lax.ppermute(v, "rows", pairs)


def always(x, z, c):
    return True


def by_x(v, d, keep=always):
    return move(v, keep, lambda x, z, c: ((x + d) % NX, z, c))


def by_z(v, d, keep=always):
    return move(v, keep, lambda x, z, c: (x, (z + d) % NZ, c))


def swap_core(v):
    return move(v, always, lambda x, z, c: (x, z, 1 - c))


GROUPS = [[rid(x, z, c) for x in range(NX) for z in range(NZ)] for c in range(2)]


def spread_static(v, x, z):
    root = (x == 0) & (z == 0)
    piece = jnp.where(root, v[0], 0.0)
    piece = piece + sum(by_x(v[d], d, lambda x, z, c: x == 0 and z == 0) for d in range(1, NX))
    piece = piece + sum(by_z(piece, d, lambda x, z, c: z == 0) for d in (2, 4, 6))
    piece = piece + by_z(piece, 1, lambda x, z, c: z % 2 == 0)
    return piece


def by_y(v, d):
    return lax.ppermute(v, "cols", [(i, (i + d) % NY) for i in range(NY)])


def gather_y(v):
    return jnp.stack([v] + [by_y(v, d) for d in range(1, NY)])


def after(value, *others):
    return lax.optimization_barrier((value,) + others)[0]


def shards(panel, window_block, row_live, window_rows):
    row = lax.axis_index("rows")
    y = lax.axis_index("cols")
    x, z, core = row // (2 * NZ), (row // 2) % NZ, row % 2

    def rows_of(i):
        return lax.dynamic_slice_in_dim(panel, i * H + y * 64, 64, 0).reshape(NX, 16, 2 * B)

    top, bot = rows_of(0), rows_of(1)
    low = lax.ppermute(bot[:, :, B:], "rows", [(1, 0)])
    first = [top[:, :, :H], bot[:, :, :H], bot[:, :, H:B], low[:, :, :H], low[:, :, H:]]
    second = [top[:, :, :H], top[:, :, H:B], bot[:, :, :H], bot[:, :, H:B], top[:, :, B : B + H]]
    stack = jnp.concatenate([jnp.where(core == 0, f, s) for f, s in zip(first, second)], axis=1)
    piece = spread_static(stack, x, z)

    width = 2 * B // NY
    mine = lax.dynamic_slice_in_dim(panel, y * width, width, 1).reshape(64, 8, width)
    chosen = pick(window_rows, lax.all_to_all(mine, "rows", 0, 0))
    piece = after(piece, *chosen)
    quarters = [chosen[0]] + [by_y(chosen[d], d) for d in range(1, NY)]
    part = jnp.stack([piece] + [by_x(piece, d) for d in range(1, NX)])

    own = gather_y(after(part, *quarters[1:]))
    other = swap_core(own)
    quarters = after(quarters, part)
    (fan,) = call(kernel_fan, 10**6, 8, [(NX * NZ, 8, 2 * B)], [], *quarters)
    t_own = lax.all_to_all(fan, "rows", 0, 0, axis_index_groups=GROUPS)

    f0, d0 = call(kernel_a, COST, 24, [(2 * B, B), (4, NB, NB)], [(2, 5 * H, H), (2 * B, B), (NB, NB)], own, other)
    t_other = swap_core(after(t_own, f0))
    f1, d1 = call(kernel_b, COST, 20, [(B, B), (4, NB, NB)], [(2, 5 * H, H), (B, B), (NB, NB)], own, other, f0)
    return call(
        kernel_c, 10**8, 60, [(B, 2 * B), (B, B)], [(2 * B, 2 * B)],
        row_live, window_rows, t_own, t_other, f0, f1, d0, d1, panel, window_block,
    )


def solution(mesh):
    in_specs = (P("rows", None), P("rows", "cols"), P(), P())
    out_specs = (P("rows", None), P("rows", "cols"))
    return jax.shard_map(shards, mesh=mesh, in_specs=in_specs, out_specs=out_specs, check_vma=False)
```

```python
import functools

import jax
import jax.numpy as jnp
from jax import lax
from jax.experimental import pallas as pl
from jax.experimental.pallas import tpu as pltpu
from jax.sharding import PartitionSpec as P

F32 = jnp.float32
B = 512
NB = 128
H = B // 2
COST = 35 * 10**8
LAST = 44
NX, NZ, NY = 4, 8, 4
CONTRACT = (((1,), (1,)), ((), ()))


def lanes(v, j):
    return jnp.broadcast_to(v[:, j : j + 1], (8, NB))


def sublanes(v, s):
    return jnp.broadcast_to(v[s : s + 1, :], (8, NB))


def factor_block(V):
    V = list(V)
    sub = lax.broadcasted_iota(jnp.int32, (8, NB), 0)
    lane = lax.broadcasted_iota(jnp.int32, (8, NB), 1)
    groups = NB // 8
    E = [jnp.where(lane == sub + 8 * k, 1.0, 0.0).astype(F32) for k in range(groups)]
    upper, inverse = [], []
    block = [lanes(V[0], b) for b in range(8)]
    for k in range(groups):
        near = list(range(k + 1, min(groups, k + 3)))
        far = list(range(k + 3, groups))
        R = [sublanes(V[k], a) for a in range(8)]
        Q = [sublanes(E[k], a) for a in range(8)]
        C = {kk: [lanes(V[kk], 8 * k + b) for b in range(8)] for kk in near}
        ahead = [lanes(V[k + 1], 8 * (k + 1) + b) for b in range(8)] if near else None
        D = {kk: [lanes(V[kk], 8 * k + b) for b in range(8)] for kk in far}
        l, invs = {}, []
        for b in range(8):
            inv = lax.rsqrt(sublanes(block[b], b))
            invs.append(inv)
            col = block[b] * inv
            for a in range(b + 1, 8):
                l[a, b] = sublanes(col, a)
            for c in range(b + 1, 8):
                block[c] = block[c] - col * l[c, b]
            for kk in near:
                C[kk][b] = C[kk][b] * inv
                for a in range(b + 1, 8):
                    C[kk][a] = C[kk][a] - C[kk][b] * l[a, b]
            if near:
                x = C[k + 1][b]
                for c in range(8):
                    ahead[c] = ahead[c] - x * sublanes(x, c)
            R[b] = R[b] * inv
            Q[b] = Q[b] * inv
            for a in range(b + 1, 8):
                R[a] = R[a] - l[a, b] * R[b]
                Q[a] = Q[a] - l[a, b] * Q[b]
            for kk in near:
                V[kk] = V[kk] - C[kk][b] * R[b]
                E[kk] = E[kk] - C[kk][b] * Q[b]
        u, x = R[0], Q[0]
        for a in range(1, 8):
            u = jnp.where(sub == a, R[a], u)
            x = jnp.where(sub == a, Q[a], x)
        upper.append(jnp.where(lane >= sub + 8 * k, u, 0.0))
        inverse.append(x)
        if far:
            W, Y = list(R), list(Q)
            for b in reversed(range(8)):
                W[b] = W[b] * invs[b]
                Y[b] = Y[b] * invs[b]
                for a in range(b):
                    W[a] = W[a] - l[b, a] * W[b]
                    Y[a] = Y[a] - l[b, a] * Y[b]
            for kk in far:
                for b in range(8):
                    V[kk] = V[kk] - D[kk][b] * W[b]
                    E[kk] = E[kk] - D[kk][b] * Y[b]
        block = ahead
    return upper, inverse


def halves(a):
    hi = a.astype(jnp.bfloat16)
    return hi, (a - hi.astype(F32)).astype(jnp.bfloat16)


def mul_t(a, b):
    ah, al = halves(a)
    bh, bl = halves(b)
    d = functools.partial(lax.dot_general, dimension_numbers=CONTRACT, preferred_element_type=F32)
    return d(ah, bh) + (d(ah, bl) + d(al, bh))


def mirrored(d):
    r = lax.broadcasted_iota(jnp.int32, (NB, NB), 0)
    c = lax.broadcasted_iota(jnp.int32, (NB, NB), 1)
    return jnp.where(r >= c, d, d.T)


def tall_factor(a_ref, f_ref, dinv_ref, d_ref):
    m, n = a_ref.shape
    nb = n // NB
    for k in range(nb):
        o = k * NB
        a_ref[o : o + NB, o : o + NB] = mirrored(a_ref[o : o + NB, o : o + NB])
    d_ref[...] = a_ref[0:NB, 0:NB]

    def body(k, carry):
        V = [d_ref[8 * i : 8 * i + 8, :] for i in range(NB // 8)]
        upper, inverse = factor_block(V)
        low = jnp.concatenate(upper, 0).T
        X = jnp.concatenate(inverse, 0)
        dinv_ref[k] = X

        def branch(kk):
            def run():
                o = NB * kk
                e = o + NB
                f_ref[o:e, o:e] = low
                if e < m:
                    Lp = mul_t(a_ref[e:, o:e], X)
                    f_ref[e:, o:e] = Lp
                if e < n:
                    f_ref[o:e, e:] = jnp.zeros((NB, n - e), F32)
                    T = a_ref[e:, e:] - mul_t(Lp, Lp[: n - e])
                    a_ref[e:, e:] = T
                    d_ref[...] = T[:NB, :NB]
                return 0

            return run

        return lax.switch(k, [branch(kk) for kk in range(nb)]) + carry

    lax.fori_loop(0, nb, body, 0)


def coords():
    row = lax.axis_index("rows")
    return row // (2 * NZ), lax.axis_index("cols"), lax.rem(row, 2)


def place(own_ref, other_ref, where):
    x, y, mine = coords()
    for dy in range(NY):
        for dx in range(NX):
            row = lax.rem(y - dy + NY, NY) * 64 + lax.rem(x - dx + NX, NX) * 16

            def put(src_ref, core):
                for b, spot in enumerate(where[core]):
                    if spot is not None:
                        ref, r, c = spot
                        at = pl.ds(pl.multiple_of(row + r, 16), 16)
                        ref[at, c : c + H] = src_ref[dy, dx, b * 16 : (b + 1) * 16]

            @pl.when(mine == 0)
            def _():
                put(own_ref, 0)
                put(other_ref, 1)

            @pl.when(mine == 1)
            def _():
                put(own_ref, 1)
                put(other_ref, 0)


def kernel_a(own_ref, other_ref, f_ref, dinv_ref, e_ref, a_ref, d_ref):
    a_ref[:H, H:] = jnp.zeros((H, H), F32)
    e_ref[:H, H:] = jnp.zeros((H, H), F32)
    first = [(a_ref, 0, 0), (a_ref, H, 0), (a_ref, H, H), (e_ref, H, 0), (e_ref, H, H)]
    second = [(a_ref, B, 0), (a_ref, B, H), (a_ref, B + H, 0), (a_ref, B + H, H), (e_ref, 0, 0)]
    place(own_ref, other_ref, [first, second])
    tall_factor(a_ref, f_ref, dinv_ref, d_ref)


def kernel_b(e_ref, f0_ref, f1_ref, dinv_ref, a_ref, d_ref):
    low = f0_ref[B:, :]
    a_ref[...] = e_ref[...] - mul_t(low, low)
    tall_factor(a_ref, f1_ref, dinv_ref, d_ref)


def pair_inverse(d_ref, j, low):
    x0, x1 = d_ref[j], d_ref[j + 1]
    corner = -mul_t(mul_t(x1, low.T), x0.T)
    top = jnp.concatenate([x0, jnp.zeros((NB, NB), F32)], axis=1)
    return jnp.concatenate([top, jnp.concatenate([corner, x1], axis=1)], axis=0)


def solve_rows(s_ref, inv, f0_ref, f1_ref):
    for k in range(4):
        o, e = k * H, (k + 1) * H
        f_ref, p = (f0_ref, o) if k < 2 else (f1_ref, o - B)
        X = mul_t(s_ref[:, o:e], inv(k))
        s_ref[:, o:e] = X
        if k < 3:
            s_ref[:, e:] = s_ref[:, e:] - mul_t(X, f_ref[p + H :, p : p + H])


def kernel_c(
    live_ref, rows_ref, f0_ref, f1_ref, d0_ref, d1_ref, own_hbm, other_hbm, panel_hbm, window_hbm,
    out_ref, factor_hbm, s_ref, t_ref, window_ref, sems,
):
    row = lax.axis_index("rows")
    _, y, mine = coords()
    panel_in = pltpu.make_async_copy(panel_hbm, s_ref.at[pl.ds(0, B)], sems.at[0])
    own_in = pltpu.make_async_copy(own_hbm, t_ref.at[0], sems.at[1])
    other_in = pltpu.make_async_copy(other_hbm, t_ref.at[1], sems.at[2])
    window_in = pltpu.make_async_copy(window_hbm, window_ref, sems.at[3])
    for c in (panel_in, own_in, other_in, window_in):
        c.start()
    inv = []
    for k in range(4):
        f_ref, d_ref, p = (f0_ref, d0_ref, k * H) if k < 2 else (f1_ref, d1_ref, k * H - B)
        inv.append(pair_inverse(d_ref, 2 * (k % 2), f_ref[p + NB : p + H, p : p + NB]))
    live_t = live_ref[rows_ref[y]].astype(F32)
    live = jnp.where(row < 2, 1, live_ref[row]).astype(F32)
    panel_in.wait()
    s_ref[:B, :] = s_ref[:B, :] * live
    own_in.wait()
    other_in.wait()
    for j in range(NX * NZ):
        s_ref[pl.ds(pl.multiple_of(B + (2 * j + mine) * 8, 8), 8), :] = t_ref[0, j] * live_t
        s_ref[pl.ds(pl.multiple_of(B + (2 * j + 1 - mine) * 8, 8), 8), :] = t_ref[1, j] * live_t
    solve_rows(s_ref, lambda k: inv[k], f0_ref, f1_ref)

    @pl.when(row == 0)
    def _():
        s_ref[:B, :B] = f0_ref[:B, :]
        s_ref[:B, B:] = jnp.zeros((B, B), F32)

    @pl.when(row == 1)
    def _():
        s_ref[:B, :B] = f0_ref[B:, :]
        s_ref[:B, B:] = f1_ref[...]

    factor_out = pltpu.make_async_copy(s_ref.at[pl.ds(0, B)], factor_hbm, sems.at[4])
    factor_out.start()
    window_in.wait()
    out_ref[...] = window_ref[...] - mul_t(s_ref[:B, :], s_ref[B:, :])
    factor_out.wait()


def kernel_pick(rows_ref, parts_ref, *refs):
    y = lax.axis_index("cols")
    outs, sems = refs[:NY], refs[NY]
    copies = [
        pltpu.make_async_copy(parts_ref.at[rows_ref[lax.rem(y + d, NY)]], outs[d], sems.at[d]) for d in range(NY)
    ]
    for c in copies:
        c.start()
    for c in copies:
        c.wait()


def kernel_fan(q0_ref, q1_ref, q2_ref, q3_ref, out_ref):
    y = lax.axis_index("cols")
    width = q0_ref.shape[1]
    for d, q_ref in enumerate((q0_ref, q1_ref, q2_ref, q3_ref)):
        at = pl.ds(pl.multiple_of(lax.rem(y - d + NY, NY) * width, width), width)
        value = q_ref[...]
        for j in range(out_ref.shape[0]):
            out_ref[j, :, at] = value


SMEM = pl.BlockSpec(memory_space=pltpu.SMEM)
VM = pl.BlockSpec(memory_space=pltpu.VMEM)


def call(kernel, flops, vmem, outs, scratch, *args):
    return pl.pallas_call(
        kernel,
        out_shape=[jax.ShapeDtypeStruct(s, F32) for s in outs],
        in_specs=[SMEM if a.dtype == jnp.int32 else VM for a in args],
        out_specs=[VM] * len(outs),
        scratch_shapes=[pltpu.VMEM(s, F32) for s in scratch],
        compiler_params=pltpu.CompilerParams(vmem_limit_bytes=vmem << 20),
        cost_estimate=pl.CostEstimate(flops=flops, transcendentals=0, bytes_accessed=8 << 20),
    )(*args)


def last(row_live, window_rows, f0, f1, d0, d1, t_own, t_other, panel, window_block):
    hbm = pl.BlockSpec(memory_space=pltpu.HBM)
    updated, factor = pl.pallas_call(
        kernel_c,
        out_shape=[jax.ShapeDtypeStruct((B, B), F32), jax.ShapeDtypeStruct((B, 2 * B), F32)],
        in_specs=[SMEM] * 2 + [VM] * 4 + [hbm] * 4,
        out_specs=[VM, hbm],
        scratch_shapes=[
            pltpu.VMEM((2 * B, 2 * B), F32),
            pltpu.VMEM((2,) + t_own.shape, F32),
            pltpu.VMEM((B, B), F32),
            pltpu.SemaphoreType.DMA((5,)),
        ],
        compiler_params=pltpu.CompilerParams(vmem_limit_bytes=LAST << 20),
    )(row_live, window_rows, f0, f1, d0, d1, t_own, t_other, panel, window_block)
    return factor, updated


def pick(window_rows, parts):
    return pl.pallas_call(
        kernel_pick,
        out_shape=[jax.ShapeDtypeStruct(parts.shape[1:], F32)] * NY,
        in_specs=[SMEM, pl.BlockSpec(memory_space=pltpu.HBM)],
        out_specs=[VM] * NY,
        scratch_shapes=[pltpu.SemaphoreType.DMA((NY,))],
        compiler_params=pltpu.CompilerParams(vmem_limit_bytes=8 << 20),
    )(window_rows, parts)


def rid(x, z, c):
    return (x * NZ + z) * 2 + c


def move(v, keep, to):
    pairs = [
        (rid(x, z, c), rid(*to(x, z, c)))
        for x in range(NX)
        for z in range(NZ)
        for c in range(2)
        if keep(x, z, c)
    ]
    return lax.ppermute(v, "rows", pairs)


def always(x, z, c):
    return True


def by_x(v, d, keep=always):
    return move(v, keep, lambda x, z, c: ((x + d) % NX, z, c))


def by_z(v, d, keep=always):
    return move(v, keep, lambda x, z, c: (x, (z + d) % NZ, c))


def swap_core(v):
    return move(v, always, lambda x, z, c: (x, z, 1 - c))


GROUPS = [[rid(x, z, c) for x in range(NX) for z in range(NZ)] for c in range(2)]


def spread_static(v, x, z):
    root = (x == 0) & (z == 0)
    piece = jnp.where(root, v[0], 0.0)
    piece = piece + sum(by_x(v[d], d, lambda x, z, c: x == 0 and z == 0) for d in range(1, NX))
    piece = piece + sum(by_z(piece, d, lambda x, z, c: z == 0) for d in (2, 4, 6))
    piece = piece + by_z(piece, 1, lambda x, z, c: z % 2 == 0)
    return piece


def by_y(v, d):
    return lax.ppermute(v, "cols", [(i, (i + d) % NY) for i in range(NY)])


def gather_y(v):
    return jnp.stack([v] + [by_y(v, d) for d in range(1, NY)])


def after(value, *others):
    return lax.optimization_barrier((value,) + others)[0]


def shards(panel, window_block, row_live, window_rows):
    row = lax.axis_index("rows")
    y = lax.axis_index("cols")
    x, z, core = row // (2 * NZ), (row // 2) % NZ, row % 2

    def rows_of(i):
        return lax.dynamic_slice_in_dim(panel, i * H + y * 64, 64, 0).reshape(NX, 16, 2 * B)

    top, bot = rows_of(0), rows_of(1)
    low = lax.ppermute(bot[:, :, B:], "rows", [(1, 0)])
    first = [top[:, :, :H], bot[:, :, :H], bot[:, :, H:B], low[:, :, :H], low[:, :, H:]]
    second = [top[:, :, :H], top[:, :, H:B], bot[:, :, :H], bot[:, :, H:B], top[:, :, B : B + H]]
    stack = jnp.concatenate([jnp.where(core == 0, f, s) for f, s in zip(first, second)], axis=1)
    piece = spread_static(stack, x, z)

    width = 2 * B // NY
    mine = lax.dynamic_slice_in_dim(panel, y * width, width, 1).reshape(64, 8, width)
    chosen = pick(window_rows, lax.all_to_all(mine, "rows", 0, 0))
    piece = after(piece, *chosen)
    quarters = [chosen[0]] + [by_y(chosen[d], d) for d in range(1, NY)]
    part = jnp.stack([piece] + [by_x(piece, d) for d in range(1, NX)])

    own = gather_y(part)
    other = swap_core(own)
    quarters = after(quarters, part)
    (fan,) = call(kernel_fan, 10**6, 8, [(NX * NZ, 8, 2 * B)], [], *quarters)
    t_own = lax.all_to_all(fan, "rows", 0, 0, axis_index_groups=GROUPS)

    f0, d0, e = call(kernel_a, COST, 24, [(2 * B, B), (4, NB, NB), (B, B)], [(2 * B, B), (NB, NB)], own, other)
    t_other = swap_core(after(t_own, f0))
    f1, d1 = call(kernel_b, COST, 20, [(B, B), (4, NB, NB)], [(B, B), (NB, NB)], e, f0)
    return last(row_live, window_rows, f0, f1, d0, d1, t_own, t_other, panel, window_block)


def solution(mesh):
    in_specs = (P("rows", None), P("rows", "cols"), P(), P())
    out_specs = (P("rows", None), P("rows", "cols"))
    return jax.shard_map(shards, mesh=mesh, in_specs=in_specs, out_specs=out_specs, check_vma=False)
```

```python
import functools

import jax
import jax.numpy as jnp
from jax import lax
from jax.experimental import pallas as pl
from jax.experimental.pallas import tpu as pltpu
from jax.sharding import PartitionSpec as P

F32 = jnp.float32
B = 512
NB = 128
H = B // 2
COST = 35 * 10**8
LAST = 44
NX, NZ, NY = 4, 8, 4
CONTRACT = (((1,), (1,)), ((), ()))


def lanes(v, j):
    return jnp.broadcast_to(v[:, j : j + 1], (8, NB))


def sublanes(v, s):
    return jnp.broadcast_to(v[s : s + 1, :], (8, NB))


def factor_block(V):
    V = list(V)
    sub = lax.broadcasted_iota(jnp.int32, (8, NB), 0)
    lane = lax.broadcasted_iota(jnp.int32, (8, NB), 1)
    groups = NB // 8
    E = [jnp.where(lane == sub + 8 * k, 1.0, 0.0).astype(F32) for k in range(groups)]
    upper, inverse = [], []
    block = [lanes(V[0], b) for b in range(8)]
    for k in range(groups):
        near = list(range(k + 1, min(groups, k + 3)))
        far = list(range(k + 3, groups))
        R = [sublanes(V[k], a) for a in range(8)]
        Q = [sublanes(E[k], a) for a in range(8)]
        C = {kk: [lanes(V[kk], 8 * k + b) for b in range(8)] for kk in near}
        ahead = [lanes(V[k + 1], 8 * (k + 1) + b) for b in range(8)] if near else None
        D = {kk: [lanes(V[kk], 8 * k + b) for b in range(8)] for kk in far}
        l, invs = {}, []
        for b in range(8):
            inv = lax.rsqrt(sublanes(block[b], b))
            invs.append(inv)
            col = block[b] * inv
            for a in range(b + 1, 8):
                l[a, b] = sublanes(col, a)
            for c in range(b + 1, 8):
                block[c] = block[c] - col * l[c, b]
            for kk in near:
                C[kk][b] = C[kk][b] * inv
                for a in range(b + 1, 8):
                    C[kk][a] = C[kk][a] - C[kk][b] * l[a, b]
            if near:
                x = C[k + 1][b]
                for c in range(8):
                    ahead[c] = ahead[c] - x * sublanes(x, c)
            R[b] = R[b] * inv
            Q[b] = Q[b] * inv
            for a in range(b + 1, 8):
                R[a] = R[a] - l[a, b] * R[b]
                Q[a] = Q[a] - l[a, b] * Q[b]
            for kk in near:
                V[kk] = V[kk] - C[kk][b] * R[b]
                E[kk] = E[kk] - C[kk][b] * Q[b]
        u, x = R[0], Q[0]
        for a in range(1, 8):
            u = jnp.where(sub == a, R[a], u)
            x = jnp.where(sub == a, Q[a], x)
        upper.append(jnp.where(lane >= sub + 8 * k, u, 0.0))
        inverse.append(x)
        if far:
            W, Y = list(R), list(Q)
            for b in reversed(range(8)):
                W[b] = W[b] * invs[b]
                Y[b] = Y[b] * invs[b]
                for a in range(b):
                    W[a] = W[a] - l[b, a] * W[b]
                    Y[a] = Y[a] - l[b, a] * Y[b]
            for kk in far:
                for b in range(8):
                    V[kk] = V[kk] - D[kk][b] * W[b]
                    E[kk] = E[kk] - D[kk][b] * Y[b]
        block = ahead
    return upper, inverse


def halves(a):
    hi = a.astype(jnp.bfloat16)
    return hi, (a - hi.astype(F32)).astype(jnp.bfloat16)


def mul_t(a, b):
    ah, al = halves(a)
    bh, bl = halves(b)
    d = functools.partial(lax.dot_general, dimension_numbers=CONTRACT, preferred_element_type=F32)
    return d(ah, bh) + (d(ah, bl) + d(al, bh))


def mirrored(d):
    r = lax.broadcasted_iota(jnp.int32, (NB, NB), 0)
    c = lax.broadcasted_iota(jnp.int32, (NB, NB), 1)
    return jnp.where(r >= c, d, d.T)


def tall_factor(a_ref, f_ref, dinv_ref, d_ref):
    m, n = a_ref.shape
    nb = n // NB
    for k in range(nb):
        o = k * NB
        a_ref[o : o + NB, o : o + NB] = mirrored(a_ref[o : o + NB, o : o + NB])
    d_ref[...] = a_ref[0:NB, 0:NB]

    def body(k, carry):
        V = [d_ref[8 * i : 8 * i + 8, :] for i in range(NB // 8)]
        upper, inverse = factor_block(V)
        low = jnp.concatenate(upper, 0).T
        X = jnp.concatenate(inverse, 0)
        dinv_ref[k] = X

        def branch(kk):
            def run():
                o = NB * kk
                e = o + NB
                f_ref[o:e, o:e] = low
                if e < m:
                    Lp = mul_t(a_ref[e:, o:e], X)
                    f_ref[e:, o:e] = Lp
                if e < n:
                    f_ref[o:e, e:] = jnp.zeros((NB, n - e), F32)
                    T = a_ref[e:, e:] - mul_t(Lp, Lp[: n - e])
                    a_ref[e:, e:] = T
                    d_ref[...] = T[:NB, :NB]
                return 0

            return run

        return lax.switch(k, [branch(kk) for kk in range(nb)]) + carry

    lax.fori_loop(0, nb, body, 0)


def coords():
    row = lax.axis_index("rows")
    return row // (2 * NZ), lax.axis_index("cols"), lax.rem(row, 2)


def place(own_ref, other_ref, where):
    x, y, mine = coords()
    for dy in range(NY):
        for dx in range(NX):
            row = lax.rem(y - dy + NY, NY) * 64 + lax.rem(x - dx + NX, NX) * 16

            def put(src_ref, core):
                for b, spot in enumerate(where[core]):
                    if spot is not None:
                        ref, r, c = spot
                        at = pl.ds(pl.multiple_of(row + r, 16), 16)
                        ref[at, c : c + H] = src_ref[dy, dx, b * 16 : (b + 1) * 16]

            @pl.when(mine == 0)
            def _():
                put(own_ref, 0)
                put(other_ref, 1)

            @pl.when(mine == 1)
            def _():
                put(own_ref, 1)
                put(other_ref, 0)


def kernel_a(own_ref, other_ref, f_ref, dinv_ref, e_ref, a_ref, d_ref):
    a_ref[:H, H:] = jnp.zeros((H, H), F32)
    e_ref[:H, H:] = jnp.zeros((H, H), F32)
    first = [(a_ref, 0, 0), (a_ref, H, 0), (a_ref, H, H), (e_ref, H, 0), (e_ref, H, H)]
    second = [(a_ref, B, 0), (a_ref, B, H), (a_ref, B + H, 0), (a_ref, B + H, H), (e_ref, 0, 0)]
    place(own_ref, other_ref, [first, second])
    tall_factor(a_ref, f_ref, dinv_ref, d_ref)


def kernel_b(e_ref, f0_ref, f1_ref, dinv_ref, a_ref, d_ref):
    low = f0_ref[B:, :]
    a_ref[...] = e_ref[...] - mul_t(low, low)
    tall_factor(a_ref, f1_ref, dinv_ref, d_ref)


def pair_inverse(d_ref, j, low):
    x0, x1 = d_ref[j], d_ref[j + 1]
    corner = -mul_t(mul_t(x1, low.T), x0.T)
    top = jnp.concatenate([x0, jnp.zeros((NB, NB), F32)], axis=1)
    return jnp.concatenate([top, jnp.concatenate([corner, x1], axis=1)], axis=0)


def solve_rows(s_ref, inv, f0_ref, f1_ref):
    for k in range(4):
        o, e = k * H, (k + 1) * H
        f_ref, p = (f0_ref, o) if k < 2 else (f1_ref, o - B)
        X = mul_t(s_ref[:, o:e], inv(k))
        s_ref[:, o:e] = X
        if k < 3:
            s_ref[:, e:] = s_ref[:, e:] - mul_t(X, f_ref[p + H :, p : p + H])


def kernel_c(
    live_ref, rows_ref, f0_ref, f1_ref, d0_ref, d1_ref, own_hbm, other_hbm, panel_hbm, window_hbm,
    out_ref, factor_hbm, s_ref, t_ref, window_ref, sems,
):
    row = lax.axis_index("rows")
    _, y, mine = coords()
    panel_in = pltpu.make_async_copy(panel_hbm, s_ref.at[pl.ds(0, B)], sems.at[0])
    own_in = pltpu.make_async_copy(own_hbm, t_ref.at[0], sems.at[1])
    other_in = pltpu.make_async_copy(other_hbm, t_ref.at[1], sems.at[2])
    window_in = pltpu.make_async_copy(window_hbm, window_ref, sems.at[3])
    for c in (panel_in, own_in, other_in, window_in):
        c.start()
    inv = []
    for k in range(4):
        f_ref, d_ref, p = (f0_ref, d0_ref, k * H) if k < 2 else (f1_ref, d1_ref, k * H - B)
        inv.append(pair_inverse(d_ref, 2 * (k % 2), f_ref[p + NB : p + H, p : p + NB]))
    live_t = live_ref[rows_ref[y]].astype(F32)
    live = jnp.where(row < 2, 1, live_ref[row]).astype(F32)
    panel_in.wait()
    s_ref[:B, :] = s_ref[:B, :] * live
    own_in.wait()
    other_in.wait()
    for j in range(NX * NZ):
        s_ref[pl.ds(pl.multiple_of(B + (2 * j + mine) * 8, 8), 8), :] = t_ref[0, j] * live_t
        s_ref[pl.ds(pl.multiple_of(B + (2 * j + 1 - mine) * 8, 8), 8), :] = t_ref[1, j] * live_t
    solve_rows(s_ref, lambda k: inv[k], f0_ref, f1_ref)

    @pl.when(row == 0)
    def _():
        s_ref[:B, :B] = f0_ref[:B, :]
        s_ref[:B, B:] = jnp.zeros((B, B), F32)

    @pl.when(row == 1)
    def _():
        s_ref[:B, :B] = f0_ref[B:, :]
        s_ref[:B, B:] = f1_ref[...]

    factor_out = pltpu.make_async_copy(s_ref.at[pl.ds(0, B)], factor_hbm, sems.at[4])
    factor_out.start()
    window_in.wait()
    out_ref[...] = window_ref[...] - mul_t(s_ref[:B, :], s_ref[B:, :])
    factor_out.wait()


def kernel_pick(rows_ref, parts_ref, *refs):
    y = lax.axis_index("cols")
    outs, sems = refs[:NY], refs[NY]
    copies = [
        pltpu.make_async_copy(parts_ref.at[rows_ref[lax.rem(y + d, NY)]], outs[d], sems.at[d]) for d in range(NY)
    ]
    for c in copies:
        c.start()
    for c in copies:
        c.wait()


def kernel_fan(q0_ref, q1_ref, q2_ref, q3_ref, out_ref):
    y = lax.axis_index("cols")
    width = q0_ref.shape[1]
    for d, q_ref in enumerate((q0_ref, q1_ref, q2_ref, q3_ref)):
        at = pl.ds(pl.multiple_of(lax.rem(y - d + NY, NY) * width, width), width)
        value = q_ref[...]
        for j in range(out_ref.shape[0]):
            out_ref[j, :, at] = value


SMEM = pl.BlockSpec(memory_space=pltpu.SMEM)
VM = pl.BlockSpec(memory_space=pltpu.VMEM)


def call(kernel, flops, vmem, outs, scratch, *args):
    return pl.pallas_call(
        kernel,
        out_shape=[jax.ShapeDtypeStruct(s, F32) for s in outs],
        in_specs=[SMEM if a.dtype == jnp.int32 else VM for a in args],
        out_specs=[VM] * len(outs),
        scratch_shapes=[pltpu.VMEM(s, F32) for s in scratch],
        compiler_params=pltpu.CompilerParams(vmem_limit_bytes=vmem << 20),
        cost_estimate=pl.CostEstimate(flops=flops, transcendentals=0, bytes_accessed=8 << 20),
    )(*args)


def last(row_live, window_rows, f0, f1, d0, d1, t_own, t_other, panel, window_block):
    hbm = pl.BlockSpec(memory_space=pltpu.HBM)
    updated, factor = pl.pallas_call(
        kernel_c,
        out_shape=[jax.ShapeDtypeStruct((B, B), F32), jax.ShapeDtypeStruct((B, 2 * B), F32)],
        in_specs=[SMEM] * 2 + [VM] * 4 + [hbm] * 4,
        out_specs=[VM, hbm],
        scratch_shapes=[
            pltpu.VMEM((2 * B, 2 * B), F32),
            pltpu.VMEM((2,) + t_own.shape, F32),
            pltpu.VMEM((B, B), F32),
            pltpu.SemaphoreType.DMA((5,)),
        ],
        compiler_params=pltpu.CompilerParams(vmem_limit_bytes=LAST << 20),
    )(row_live, window_rows, f0, f1, d0, d1, t_own, t_other, panel, window_block)
    return factor, updated


def pick(window_rows, parts):
    return pl.pallas_call(
        kernel_pick,
        out_shape=[jax.ShapeDtypeStruct(parts.shape[1:], F32)] * NY,
        in_specs=[SMEM, pl.BlockSpec(memory_space=pltpu.HBM)],
        out_specs=[VM] * NY,
        scratch_shapes=[pltpu.SemaphoreType.DMA((NY,))],
        compiler_params=pltpu.CompilerParams(vmem_limit_bytes=8 << 20),
    )(window_rows, parts)


def rid(x, z, c):
    return (x * NZ + z) * 2 + c


def move(v, keep, to):
    pairs = [
        (rid(x, z, c), rid(*to(x, z, c)))
        for x in range(NX)
        for z in range(NZ)
        for c in range(2)
        if keep(x, z, c)
    ]
    return lax.ppermute(v, "rows", pairs)


def always(x, z, c):
    return True


def by_x(v, d, keep=always):
    return move(v, keep, lambda x, z, c: ((x + d) % NX, z, c))


def by_z(v, d, keep=always):
    return move(v, keep, lambda x, z, c: (x, (z + d) % NZ, c))


def swap_core(v):
    return move(v, always, lambda x, z, c: (x, z, 1 - c))


GROUPS = [[rid(x, z, c) for x in range(NX) for z in range(NZ)] for c in range(2)]


def spread_static(v, x, z):
    root = (x == 0) & (z == 0)
    piece = jnp.where(root, v[0], 0.0)
    piece = piece + sum(by_x(v[d], d, lambda x, z, c: x == 0 and z == 0) for d in range(1, NX))
    piece = piece + sum(by_z(piece, d, lambda x, z, c: z == 0) for d in (2, 4, 6))
    piece = piece + by_z(piece, 1, lambda x, z, c: z % 2 == 0)
    return piece


def by_y(v, d):
    return lax.ppermute(v, "cols", [(i, (i + d) % NY) for i in range(NY)])


def gather_y(v):
    return jnp.stack([v] + [by_y(v, d) for d in range(1, NY)])


def after(value, *others):
    return lax.optimization_barrier((value,) + others)[0]


def shards(panel, window_block, row_live, window_rows):
    row = lax.axis_index("rows")
    y = lax.axis_index("cols")
    x, z, core = row // (2 * NZ), (row // 2) % NZ, row % 2

    def rows_of(i):
        return lax.dynamic_slice_in_dim(panel, i * H + y * 64, 64, 0).reshape(NX, 16, 2 * B)

    top, bot = rows_of(0), rows_of(1)
    low = lax.ppermute(bot[:, :, B:], "rows", [(1, 0)])
    first = [top[:, :, :H], bot[:, :, :H], bot[:, :, H:B], low[:, :, :H], low[:, :, H:]]
    second = [top[:, :, :H], top[:, :, H:B], bot[:, :, :H], bot[:, :, H:B], top[:, :, B : B + H]]
    stack = jnp.concatenate([jnp.where(core == 0, f, s) for f, s in zip(first, second)], axis=1)
    piece = spread_static(stack, x, z)

    width = 2 * B // NY
    mine = lax.dynamic_slice_in_dim(panel, y * width, width, 1).reshape(64, 8, width)
    chosen = pick(window_rows, lax.all_to_all(mine, "rows", 0, 0))
    piece = after(piece, *chosen)
    quarters = [chosen[0]] + [by_y(chosen[d], d) for d in range(1, NY)]
    part = jnp.stack([piece] + [by_x(piece, d) for d in range(1, NX)])

    own = gather_y(after(part, *quarters[1:]))
    other = swap_core(own)
    quarters = after(quarters, part)
    (fan,) = call(kernel_fan, 10**6, 8, [(NX * NZ, 8, 2 * B)], [], *quarters)
    t_own = lax.all_to_all(fan, "rows", 0, 0, axis_index_groups=GROUPS)

    f0, d0, e = call(kernel_a, COST, 24, [(2 * B, B), (4, NB, NB), (B, B)], [(2 * B, B), (NB, NB)], own, other)
    t_other = swap_core(after(t_own, f0))
    f1, d1 = call(kernel_b, COST, 20, [(B, B), (4, NB, NB)], [(B, B), (NB, NB)], e, f0)
    return last(row_live, window_rows, f0, f1, d0, d1, t_own, t_other, panel, window_block)


def solution(mesh):
    in_specs = (P("rows", None), P("rows", "cols"), P(), P())
    out_specs = (P("rows", None), P("rows", "cols"))
    return jax.shard_map(shards, mesh=mesh, in_specs=in_specs, out_specs=out_specs, check_vma=False)
```

```python
import functools

import jax
import jax.numpy as jnp
from jax import lax
from jax.experimental import pallas as pl
from jax.experimental.pallas import tpu as pltpu
from jax.sharding import PartitionSpec as P

F32 = jnp.float32
B = 512
NB = 128
H = B // 2
COST = 35 * 10**8
LAST = 44
NX, NZ, NY = 4, 8, 4
CONTRACT = (((1,), (1,)), ((), ()))


def lanes(v, j):
    return jnp.broadcast_to(v[:, j : j + 1], (8, NB))


def sublanes(v, s):
    return jnp.broadcast_to(v[s : s + 1, :], (8, NB))


def factor_block(V):
    V = list(V)
    sub = lax.broadcasted_iota(jnp.int32, (8, NB), 0)
    lane = lax.broadcasted_iota(jnp.int32, (8, NB), 1)
    groups = NB // 8
    E = [jnp.where(lane == sub + 8 * k, 1.0, 0.0).astype(F32) for k in range(groups)]
    upper, inverse = [], []
    block = [lanes(V[0], b) for b in range(8)]
    for k in range(groups):
        near = list(range(k + 1, min(groups, k + 3)))
        far = list(range(k + 3, groups))
        R = [sublanes(V[k], a) for a in range(8)]
        Q = [sublanes(E[k], a) for a in range(8)]
        C = {kk: [lanes(V[kk], 8 * k + b) for b in range(8)] for kk in near}
        ahead = [lanes(V[k + 1], 8 * (k + 1) + b) for b in range(8)] if near else None
        D = {kk: [lanes(V[kk], 8 * k + b) for b in range(8)] for kk in far}
        l, invs = {}, []
        for b in range(8):
            inv = lax.rsqrt(sublanes(block[b], b))
            invs.append(inv)
            col = block[b] * inv
            for a in range(b + 1, 8):
                l[a, b] = sublanes(col, a)
            for c in range(b + 1, 8):
                block[c] = block[c] - col * l[c, b]
            for kk in near:
                C[kk][b] = C[kk][b] * inv
                for a in range(b + 1, 8):
                    C[kk][a] = C[kk][a] - C[kk][b] * l[a, b]
            if near:
                x = C[k + 1][b]
                for c in range(8):
                    ahead[c] = ahead[c] - x * sublanes(x, c)
            R[b] = R[b] * inv
            Q[b] = Q[b] * inv
            for a in range(b + 1, 8):
                R[a] = R[a] - l[a, b] * R[b]
                Q[a] = Q[a] - l[a, b] * Q[b]
            for kk in near:
                V[kk] = V[kk] - C[kk][b] * R[b]
                E[kk] = E[kk] - C[kk][b] * Q[b]
        u, x = R[0], Q[0]
        for a in range(1, 8):
            u = jnp.where(sub == a, R[a], u)
            x = jnp.where(sub == a, Q[a], x)
        upper.append(jnp.where(lane >= sub + 8 * k, u, 0.0))
        inverse.append(x)
        if far:
            W, Y = list(R), list(Q)
            for b in reversed(range(8)):
                W[b] = W[b] * invs[b]
                Y[b] = Y[b] * invs[b]
                for a in range(b):
                    W[a] = W[a] - l[b, a] * W[b]
                    Y[a] = Y[a] - l[b, a] * Y[b]
            for kk in far:
                for b in range(8):
                    V[kk] = V[kk] - D[kk][b] * W[b]
                    E[kk] = E[kk] - D[kk][b] * Y[b]
        block = ahead
    return upper, inverse


def halves(a):
    hi = a.astype(jnp.bfloat16)
    return hi, (a - hi.astype(F32)).astype(jnp.bfloat16)


def mul_t(a, b):
    ah, al = halves(a)
    bh, bl = halves(b)
    d = functools.partial(lax.dot_general, dimension_numbers=CONTRACT, preferred_element_type=F32)
    return d(ah, bh) + (d(ah, bl) + d(al, bh))


def mirrored(d):
    r = lax.broadcasted_iota(jnp.int32, (NB, NB), 0)
    c = lax.broadcasted_iota(jnp.int32, (NB, NB), 1)
    return jnp.where(r >= c, d, d.T)


def tall_factor(a_ref, f_ref, dinv_ref, d_ref):
    m, n = a_ref.shape
    nb = n // NB
    for k in range(nb):
        o = k * NB
        a_ref[o : o + NB, o : o + NB] = mirrored(a_ref[o : o + NB, o : o + NB])
    d = a_ref[0:NB, 0:NB]
    held = None
    for k in range(nb):
        o = k * NB
        e = o + NB
        if held is not None and e < m:
            X, below = held
            Lp = mul_t(a_ref[e:, o - NB : o], X)
            f_ref[e:m, o - NB : o] = Lp
            a_ref[e:, o:e] = a_ref[e:, o:e] - mul_t(Lp, below)
            if e < n:
                a_ref[e:, e:] = a_ref[e:, e:] - mul_t(Lp, Lp[: n - e])
        upper, inverse = factor_block([d[8 * i : 8 * i + 8, :] for i in range(NB // 8)])
        X = jnp.concatenate(inverse, 0)
        dinv_ref[k] = X
        f_ref[o:e, o:e] = jnp.concatenate(upper, 0).T
        if e < n:
            f_ref[o:e, e:] = jnp.zeros((NB, n - e), F32)
            below = mul_t(a_ref[e : e + NB, o:e], X)
            f_ref[e : e + NB, o:e] = below
            d = a_ref[e : e + NB, e : e + NB] - mul_t(below, below)
            held = X, below
        elif e < m:
            f_ref[e:m, o:e] = mul_t(a_ref[e:, o:e], X)


def coords():
    row = lax.axis_index("rows")
    return row // (2 * NZ), lax.axis_index("cols"), lax.rem(row, 2)


def place(own_ref, other_ref, where):
    x, y, mine = coords()
    for dy in range(NY):
        for dx in range(NX):
            row = lax.rem(y - dy + NY, NY) * 64 + lax.rem(x - dx + NX, NX) * 16

            def put(src_ref, core):
                for b, spot in enumerate(where[core]):
                    if spot is not None:
                        ref, r, c = spot
                        at = pl.ds(pl.multiple_of(row + r, 16), 16)
                        ref[at, c : c + H] = src_ref[dy, dx, b * 16 : (b + 1) * 16]

            @pl.when(mine == 0)
            def _():
                put(own_ref, 0)
                put(other_ref, 1)

            @pl.when(mine == 1)
            def _():
                put(own_ref, 1)
                put(other_ref, 0)


def kernel_a(own_ref, other_ref, f_ref, dinv_ref, e_ref, a_ref, d_ref):
    a_ref[:H, H:] = jnp.zeros((H, H), F32)
    e_ref[:H, H:] = jnp.zeros((H, H), F32)
    first = [(a_ref, 0, 0), (a_ref, H, 0), (a_ref, H, H), (e_ref, H, 0), (e_ref, H, H)]
    second = [(a_ref, B, 0), (a_ref, B, H), (a_ref, B + H, 0), (a_ref, B + H, H), (e_ref, 0, 0)]
    place(own_ref, other_ref, [first, second])
    tall_factor(a_ref, f_ref, dinv_ref, d_ref)


def kernel_b(e_ref, f0_ref, f1_ref, dinv_ref, a_ref, d_ref):
    low = f0_ref[B:, :]
    a_ref[...] = e_ref[...] - mul_t(low, low)
    tall_factor(a_ref, f1_ref, dinv_ref, d_ref)


def pair_inverse(d_ref, j, low):
    x0, x1 = d_ref[j], d_ref[j + 1]
    corner = -mul_t(mul_t(x1, low.T), x0.T)
    top = jnp.concatenate([x0, jnp.zeros((NB, NB), F32)], axis=1)
    return jnp.concatenate([top, jnp.concatenate([corner, x1], axis=1)], axis=0)


def solve_rows(s_ref, inv, f0_ref, f1_ref):
    for k in range(4):
        o, e = k * H, (k + 1) * H
        f_ref, p = (f0_ref, o) if k < 2 else (f1_ref, o - B)
        X = mul_t(s_ref[:, o:e], inv(k))
        s_ref[:, o:e] = X
        if k < 3:
            s_ref[:, e:] = s_ref[:, e:] - mul_t(X, f_ref[p + H :, p : p + H])


def kernel_c(
    live_ref, rows_ref, f0_ref, f1_ref, d0_ref, d1_ref, own_hbm, other_hbm, panel_hbm, window_hbm,
    out_ref, factor_hbm, s_ref, t_ref, window_ref, sems,
):
    row = lax.axis_index("rows")
    _, y, mine = coords()
    panel_in = pltpu.make_async_copy(panel_hbm, s_ref.at[pl.ds(0, B)], sems.at[0])
    own_in = pltpu.make_async_copy(own_hbm, t_ref.at[0], sems.at[1])
    other_in = pltpu.make_async_copy(other_hbm, t_ref.at[1], sems.at[2])
    window_in = pltpu.make_async_copy(window_hbm, window_ref, sems.at[3])
    for c in (panel_in, own_in, other_in, window_in):
        c.start()
    inv = []
    for k in range(4):
        f_ref, d_ref, p = (f0_ref, d0_ref, k * H) if k < 2 else (f1_ref, d1_ref, k * H - B)
        inv.append(pair_inverse(d_ref, 2 * (k % 2), f_ref[p + NB : p + H, p : p + NB]))
    live_t = live_ref[rows_ref[y]].astype(F32)
    live = jnp.where(row < 2, 1, live_ref[row]).astype(F32)
    panel_in.wait()
    s_ref[:B, :] = s_ref[:B, :] * live
    own_in.wait()
    other_in.wait()
    for j in range(NX * NZ):
        s_ref[pl.ds(pl.multiple_of(B + (2 * j + mine) * 8, 8), 8), :] = t_ref[0, j] * live_t
        s_ref[pl.ds(pl.multiple_of(B + (2 * j + 1 - mine) * 8, 8), 8), :] = t_ref[1, j] * live_t
    solve_rows(s_ref, lambda k: inv[k], f0_ref, f1_ref)

    @pl.when(row == 0)
    def _():
        s_ref[:B, :B] = f0_ref[:B, :]
        s_ref[:B, B:] = jnp.zeros((B, B), F32)

    @pl.when(row == 1)
    def _():
        s_ref[:B, :B] = f0_ref[B:, :]
        s_ref[:B, B:] = f1_ref[...]

    factor_out = pltpu.make_async_copy(s_ref.at[pl.ds(0, B)], factor_hbm, sems.at[4])
    factor_out.start()
    window_in.wait()
    out_ref[...] = window_ref[...] - mul_t(s_ref[:B, :], s_ref[B:, :])
    factor_out.wait()


def kernel_pick(rows_ref, parts_ref, *refs):
    y = lax.axis_index("cols")
    outs, sems = refs[:NY], refs[NY]
    copies = [
        pltpu.make_async_copy(parts_ref.at[rows_ref[lax.rem(y + d, NY)]], outs[d], sems.at[d]) for d in range(NY)
    ]
    for c in copies:
        c.start()
    for c in copies:
        c.wait()


def kernel_fan(q0_ref, q1_ref, q2_ref, q3_ref, out_ref):
    y = lax.axis_index("cols")
    width = q0_ref.shape[1]
    for d, q_ref in enumerate((q0_ref, q1_ref, q2_ref, q3_ref)):
        at = pl.ds(pl.multiple_of(lax.rem(y - d + NY, NY) * width, width), width)
        value = q_ref[...]
        for j in range(out_ref.shape[0]):
            out_ref[j, :, at] = value


SMEM = pl.BlockSpec(memory_space=pltpu.SMEM)
VM = pl.BlockSpec(memory_space=pltpu.VMEM)


def call(kernel, flops, vmem, outs, scratch, *args):
    return pl.pallas_call(
        kernel,
        out_shape=[jax.ShapeDtypeStruct(s, F32) for s in outs],
        in_specs=[SMEM if a.dtype == jnp.int32 else VM for a in args],
        out_specs=[VM] * len(outs),
        scratch_shapes=[pltpu.VMEM(s, F32) for s in scratch],
        compiler_params=pltpu.CompilerParams(vmem_limit_bytes=vmem << 20),
        cost_estimate=pl.CostEstimate(flops=flops, transcendentals=0, bytes_accessed=8 << 20),
    )(*args)


def last(row_live, window_rows, f0, f1, d0, d1, t_own, t_other, panel, window_block):
    hbm = pl.BlockSpec(memory_space=pltpu.HBM)
    updated, factor = pl.pallas_call(
        kernel_c,
        out_shape=[jax.ShapeDtypeStruct((B, B), F32), jax.ShapeDtypeStruct((B, 2 * B), F32)],
        in_specs=[SMEM] * 2 + [VM] * 4 + [hbm] * 4,
        out_specs=[VM, hbm],
        scratch_shapes=[
            pltpu.VMEM((2 * B, 2 * B), F32),
            pltpu.VMEM((2,) + t_own.shape, F32),
            pltpu.VMEM((B, B), F32),
            pltpu.SemaphoreType.DMA((5,)),
        ],
        compiler_params=pltpu.CompilerParams(vmem_limit_bytes=LAST << 20),
    )(row_live, window_rows, f0, f1, d0, d1, t_own, t_other, panel, window_block)
    return factor, updated


def pick(window_rows, parts):
    return pl.pallas_call(
        kernel_pick,
        out_shape=[jax.ShapeDtypeStruct(parts.shape[1:], F32)] * NY,
        in_specs=[SMEM, pl.BlockSpec(memory_space=pltpu.HBM)],
        out_specs=[VM] * NY,
        scratch_shapes=[pltpu.SemaphoreType.DMA((NY,))],
        compiler_params=pltpu.CompilerParams(vmem_limit_bytes=8 << 20),
    )(window_rows, parts)


def rid(x, z, c):
    return (x * NZ + z) * 2 + c


def move(v, keep, to):
    pairs = [
        (rid(x, z, c), rid(*to(x, z, c)))
        for x in range(NX)
        for z in range(NZ)
        for c in range(2)
        if keep(x, z, c)
    ]
    return lax.ppermute(v, "rows", pairs)


def always(x, z, c):
    return True


def by_x(v, d, keep=always):
    return move(v, keep, lambda x, z, c: ((x + d) % NX, z, c))


def by_z(v, d, keep=always):
    return move(v, keep, lambda x, z, c: (x, (z + d) % NZ, c))


def swap_core(v):
    return move(v, always, lambda x, z, c: (x, z, 1 - c))


GROUPS = [[rid(x, z, c) for x in range(NX) for z in range(NZ)] for c in range(2)]


def spread_static(v, x, z):
    root = (x == 0) & (z == 0)
    piece = jnp.where(root, v[0], 0.0)
    piece = piece + sum(by_x(v[d], d, lambda x, z, c: x == 0 and z == 0) for d in range(1, NX))
    piece = piece + sum(by_z(piece, d, lambda x, z, c: z == 0) for d in (2, 4, 6))
    piece = piece + by_z(piece, 1, lambda x, z, c: z % 2 == 0)
    return piece


def by_y(v, d):
    return lax.ppermute(v, "cols", [(i, (i + d) % NY) for i in range(NY)])


def gather_y(v):
    return jnp.stack([v] + [by_y(v, d) for d in range(1, NY)])


def after(value, *others):
    return lax.optimization_barrier((value,) + others)[0]


def shards(panel, window_block, row_live, window_rows):
    row = lax.axis_index("rows")
    y = lax.axis_index("cols")
    x, z, core = row // (2 * NZ), (row // 2) % NZ, row % 2

    def rows_of(i):
        return lax.dynamic_slice_in_dim(panel, i * H + y * 64, 64, 0).reshape(NX, 16, 2 * B)

    top, bot = rows_of(0), rows_of(1)
    low = lax.ppermute(bot[:, :, B:], "rows", [(1, 0)])
    first = [top[:, :, :H], bot[:, :, :H], bot[:, :, H:B], low[:, :, :H], low[:, :, H:]]
    second = [top[:, :, :H], top[:, :, H:B], bot[:, :, :H], bot[:, :, H:B], top[:, :, B : B + H]]
    stack = jnp.concatenate([jnp.where(core == 0, f, s) for f, s in zip(first, second)], axis=1)
    piece = spread_static(stack, x, z)

    width = 2 * B // NY
    mine = lax.dynamic_slice_in_dim(panel, y * width, width, 1).reshape(64, 8, width)
    chosen = pick(window_rows, lax.all_to_all(mine, "rows", 0, 0))
    piece = after(piece, *chosen)
    quarters = [chosen[0]] + [by_y(chosen[d], d) for d in range(1, NY)]
    part = jnp.stack([piece] + [by_x(piece, d) for d in range(1, NX)])

    own = gather_y(after(part, *quarters[1:]))
    other = swap_core(own)
    quarters = after(quarters, part)
    (fan,) = call(kernel_fan, 10**6, 8, [(NX * NZ, 8, 2 * B)], [], *quarters)
    t_own = lax.all_to_all(fan, "rows", 0, 0, axis_index_groups=GROUPS)

    f0, d0, e = call(kernel_a, COST, 24, [(2 * B, B), (4, NB, NB), (B, B)], [(2 * B, B), (NB, NB)], own, other)
    t_other = swap_core(after(t_own, f0))
    f1, d1 = call(kernel_b, COST, 20, [(B, B), (4, NB, NB)], [(B, B), (NB, NB)], e, f0)
    return last(row_live, window_rows, f0, f1, d0, d1, t_own, t_other, panel, window_block)


def solution(mesh):
    in_specs = (P("rows", None), P("rows", "cols"), P(), P())
    out_specs = (P("rows", None), P("rows", "cols"))
    return jax.shard_map(shards, mesh=mesh, in_specs=in_specs, out_specs=out_specs, check_vma=False)
```
